256 devices in a mesh: rows: 16 (over x_lo, y, core), labels: 16 (over z, x_hi).
Axes of the slice: x: 4 (x_hi: 2, x_lo: 2; x = x_hi * 2 + x_lo), y: 4, z: 8, core: 2. Of those that a mesh axis runs over, the one named last changes fastest.
Arguments:
- points: bfloat16 [8192, 1024], P('rows'), may hold values from -6 to 6
- targets: bfloat16 [8192, 21504], P('rows', 'labels'), may hold values from -6 to 6
- coeffs: float32 [8192, 21504], P('rows', 'labels'), may hold values from -6 to 6
- block_ids: int32 [2, 512], replicated, may hold values from 0 to 8191, as said below
- inverses: float32 [2, 512, 512], replicated, as said below
Outputs:
- new_coeffs: float32 [8192, 21504], P('rows', 'labels')
The draws below stay inside these ranges and needn't reach their ends.
Inputs may be any that keep to these rules, and one draw needn't show every extreme that they name: `block_ids`: the 512 ids of one block are distinct; the two blocks may share ids. Each inverses[b] is symmetric with a positive diagonal.
All inputs are finite; a program needn't handle non-finite values.
Results may differ from the reference program's by a relative error of at most 0.0029.
Values may be sent and summed in bfloat16 or wider, within the bound.
A program may use at most 64 MiB of HBM per device.

```python
import jax
import jax.numpy as jnp
from jax import lax

FEAT = 1024
LABELS = 21504
BLOCK = 512
NPTS = 8192


def draw_block_ids(key, part):
    quarter = NPTS // 4
    half_block = BLOCK // 2
    blocks_out = []
    for blk in range(2):
        sub_key = jax.random.fold_in(key, 11 + blk)
        key_one, key_two, key_three = jax.random.split(sub_key, 3)
        which = jax.random.randint(key_one, (), 0, 4)
        clustered = jax.random.permutation(key_two, quarter)[:half_block] + which * quarter
        spread = (jax.random.permutation(key_three, NPTS - quarter)[:BLOCK - half_block] + (which + 1) * quarter) % NPTS
        blocks_out.append(jnp.concatenate([clustered, spread]).astype(jnp.int32))
    return jnp.stack(blocks_out).astype(jnp.int32)


def draw_inverses(key, part):
    key_one, key_two = jax.random.split(jax.random.fold_in(key, 5))
    off_scale = 0.3
    diag_vals = jax.random.uniform(key_two, (2, BLOCK), jnp.float32, 0.5, 1.0)
    base = jax.random.normal(key_one, (2, BLOCK, BLOCK), jnp.float32) * (off_scale / BLOCK ** 0.5)
    symmetric = (base + jnp.swapaxes(base, 1, 2)) * 0.7071067811865476
    eye_mat = jnp.eye(BLOCK, dtype=jnp.float32)
    return (symmetric * (1.0 - eye_mat) + eye_mat[None] * diag_vals[:, :, None]).astype(jnp.float32)


def shard_levels(rng, shape, shards, least, largest):
    loudness, own = 1.0, jax.random.fold_in(rng, 6)
    for dim, parts in shards:
        heights = jnp.exp(jax.random.uniform(jax.random.fold_in(own, dim), (parts,), jnp.float32, least / len(shards), largest / len(shards)))
        loudness = loudness * jnp.repeat(heights, shape[dim] // parts).reshape([-1 if axis == dim else 1 for axis in range(len(shape))])
    return loudness


def bell_draw(key, shape, scale, reach, cuts=(), held_as=jnp.bfloat16):
    drawn = jax.random.normal(key, shape, jnp.float32) * scale
    if len(cuts) > 0:
        drawn = shard_levels(key, shape, cuts, -0.22, 0.18) * drawn
    return jnp.clip(drawn, min=-reach, max=reach).astype(held_as)


def setup_inputs(seed: int = 0) -> dict:
    keys = jax.random.split(jax.random.key(seed), 6)
    return {
        "points": bell_draw(keys[0], (NPTS, FEAT), 1.0, 6.0, ((0, 16),)),
        "targets": bell_draw(keys[1], (NPTS, LABELS), 1.0, 6.0, ((0, 16), (1, 16))),
        "coeffs": bell_draw(keys[2], (NPTS, LABELS), 1.0, 6.0, ((0, 16), (1, 16)), jnp.float32),
        "block_ids": draw_block_ids(jax.random.fold_in(keys[5], 71), 0),
        "inverses": draw_inverses(jax.random.fold_in(keys[5], 71), 0),
    }


ridge_weight = 0.5


def kernel_tile(left, right):
    inner_prod = lax.dot_general(left, right, (((1,), (1,)), ((), ())), preferred_element_type=jnp.float32)
    left_sq = jnp.sum(jnp.square(left.astype(jnp.float32)), axis=1)
    right_sq = jnp.sum(jnp.square(right.astype(jnp.float32)), axis=1)
    sq_dist = jnp.maximum(left_sq[:, None] + right_sq[None, :] - 2.0 * inner_prod, 0.0)
    return jnp.exp(-(2.0 / left.shape[1]) * sq_dist).astype(jnp.bfloat16)


def reference(points, targets, coeffs, block_ids, inverses):
    current = coeffs
    for blk in range(2):
        point_ids = block_ids[blk].astype(jnp.int32)
        block_pts = points[point_ids]
        ktile = kernel_tile(points, block_pts)
        c_low = current.astype(jnp.bfloat16)
        product = lax.dot_general(ktile, c_low, (((0,), (0,)), ((), ())), preferred_element_type=jnp.float32)
        resid = targets[point_ids].astype(jnp.float32) - product - ridge_weight * current[point_ids]
        update = jnp.dot(inverses[blk], resid, precision=lax.Precision.HIGHEST, preferred_element_type=jnp.float32)
        current = current.at[point_ids].add(update)
    return current
```

```python
import functools

import jax
import jax.numpy as jnp
from jax import lax
from jax.experimental import pallas as pl
from jax.experimental.pallas import tpu as pltpu
from jax.sharding import PartitionSpec as P

RIDGE = 0.5
MESH = pl.DeviceIdType.MESH
F32, BF16 = jnp.float32, jnp.bfloat16
LANES = 128
WIDE = 512
COPIES = 160
NT = (((1,), (1,)), ((), ()))


def mm(a, b):
    return jnp.dot(a, b, preferred_element_type=F32)


def mm_nt(a, b):
    return lax.dot_general(a, b, NT, preferred_element_type=F32)


def split(x):
    hi = x.astype(BF16)
    return hi, (x - hi.astype(F32)).astype(BF16)


def one_hot(a, b):
    return jnp.where(a == b, 1.0, 0.0)


def row_norms(x):
    hi, lo = split(jnp.square(x.astype(F32)))
    ones = jnp.ones((8, x.shape[1]), BF16)
    return (mm_nt(ones, hi) + mm_nt(ones, lo))[0:1]


def gauss(left, right, right_norms):
    left_norms = jnp.sum(jnp.square(left.astype(F32)), axis=1, keepdims=True)
    dist = jnp.maximum(left_norms + right_norms - 2.0 * mm_nt(left, right), 0.0)
    return jnp.exp(-(2.0 / left.shape[1]) * dist).astype(BF16)


def body(cols, points, col_ids, row_ids, targets_hbm, coeffs_hbm, inverses_hbm, out_hbm, *scratch):
    n_chunks = len(cols)
    (targets, coeffs, inverses, c_low, ko, qx_send, qx_recv, qchip, qr_recv, qpiece, qbuf,
     gb_hi, gb_lo, g1_hi, g1_lo, load_sem, store_sem, send_sem, recv_sem) = scratch[:19]
    names = ("p_send", "p_own", "p_recv", "far", "rfar", "near", "rnear", "xs", "xr", "rbuf", "outv")
    bufs = [dict(zip(names, scratch[19 + len(names) * j: 19 + len(names) * (j + 1)])) for j in range(n_chunks)]

    me = lax.axis_index("rows")
    lab = lax.axis_index("labels")
    core = me % 2
    chip = me // 2
    y = chip % 4
    x = chip // 4
    z = lab // 2
    xh = lab % 2
    half = ko.shape[0] // 2
    local = points.shape[0]

    def chip_peer(d):
        return {"rows": ((chip + d) % 8) * 2 + core}

    partner = {"rows": chip * 2 + 1 - core}
    y_up = {"rows": (x * 4 + (y + 1) % 4) * 2 + core}
    y_dn = {"rows": (x * 4 + (y + 3) % 4) * 2 + core}
    x_nb = {"rows": ((1 - x) * 4 + y) * 2 + core}
    z_up = {"labels": ((z + 1) % 8) * 2 + xh}
    z_dn = {"labels": ((z + 7) % 8) * 2 + xh}

    loads = [
        pltpu.make_async_copy(coeffs_hbm, coeffs, load_sem.at[0]),
        pltpu.make_async_copy(targets_hbm, targets, load_sem.at[1]),
        pltpu.make_async_copy(inverses_hbm, inverses, load_sem.at[2]),
    ]
    for ld in loads:
        ld.start()

    barrier = pltpu.get_barrier_semaphore()
    greet = [partner, z_up, z_dn] + [chip_peer(d) for d in range(1, 8)]
    for dev in greet:
        pl.semaphore_signal(barrier, inc=1, device_id=dev, device_id_type=MESH)

    sent = []

    def push(src, dst, dev):
        i = len(sent)
        cp = pltpu.make_async_remote_copy(
            src_ref=src, dst_ref=dst, send_sem=send_sem.at[i], recv_sem=recv_sem.at[i],
            device_id=dev, device_id_type=MESH)
        cp.start()
        sent.append(cp)
        return cp

    first_row = me * local
    lane_row = first_row + lax.broadcasted_iota(jnp.int32, (1, local), 1)

    def picked(which):
        base = pl.multiple_of(z * 128 + which * 64, 64)
        sel = one_hot(col_ids[pl.ds(base, 64), :], lane_row).astype(BF16)
        return mm(sel, points[...])

    theirs = picked(1 - core).astype(BF16)
    for f in range(8):
        qx_send[f] = theirs[:, f * LANES:(f + 1) * LANES]
    pl.semaphore_wait(barrier, len(greet))
    qx = push(qx_send, qx_recv, partner)
    mine = picked(core)
    qx.wait_recv()
    for f in range(8):
        qchip[f] = (mine[:, f * LANES:(f + 1) * LANES] + qx_recv[f].astype(F32)).astype(BF16)
    red = [push(qchip.at[(chip + d) % 8], qr_recv.at[d - 1], chip_peer(d)) for d in range(1, 8)]

    point_norms = row_norms(points[...])
    loads[0].wait()
    c_low[...] = coeffs[...].astype(BF16)

    piece = qchip[chip].astype(F32)
    for d in range(1, 8):
        red[d - 1].wait_recv()
        piece = piece + qr_recv[d - 1].astype(F32)
    qpiece[...] = piece.astype(BF16)
    zrows = pl.ds(pl.multiple_of(z * 128 + core * 64, 64), 64)
    qbuf[chip, zrows, :] = piece.astype(BF16)
    gat = [push(qpiece, qbuf.at[chip, zrows, :], chip_peer(d)) for d in range(1, 8)]
    for cp in gat:
        cp.wait_recv()

    def zchunk(zz, h):
        rows = pl.ds(pl.multiple_of((zz % 8) * 128 + core * 64, 64), 64)
        ref = qbuf.at[pl.ds(4 * h, 4), rows, :]
        return ref

    shares = []

    def share_q(zz, h):
        shares.append(push(zchunk(zz, h), zchunk(zz, h), partner))

    hops = {}
    for s in range(1, 5):
        for h in range(2):
            for sign, dev in ((1, z_up), (-1, z_dn)):
                if s == 4 and (h == 0) != (sign == 1):
                    continue
                if s > 1:
                    hops[sign, s - 1, h].wait_recv()
                held = z + 8 - sign * (s - 1)
                hops[sign, s, h] = push(zchunk(held, h), zchunk(held, h), dev)
                if s == 1 and sign == 1:
                    share_q(z, h)
                elif s > 1:
                    share_q(held, h)
                if s == 4:
                    hops[sign, 3, 1 - h].wait_recv()
                    share_q(held, 1 - h)
        if s == 1:
            row = first_row + lax.broadcasted_iota(jnp.int32, (local, 1), 0)
            loads[2].wait()
            sel_t0 = one_hot(row, row_ids[:, :half]).astype(BF16)
            hi, lo = split(inverses[0])
            gb_hi[:local, :] = mm(sel_t0, hi).astype(BF16)
            gb_lo[:local, :] = mm(sel_t0, lo).astype(BF16)
        if s == 2:
            sel_t1 = one_hot(row, row_ids[:, half:]).astype(BF16)
            hi, lo = split(inverses[1])
            g1_hi[...] = mm(sel_t1, hi).astype(BF16)
            g1_lo[...] = mm(sel_t1, lo).astype(BF16)
            loads[1].wait()
    hops[1, 4, 0].wait_recv()
    share_q(z + 4, 0)
    hops[-1, 4, 1].wait_recv()
    share_q(z + 4, 1)
    for cp in shares:
        cp.wait_recv()

    def block_points(start, size):
        return jnp.concatenate([qbuf[f, pl.ds(start, size), :] for f in range(8)], axis=1)

    def left_operand(m, carry):
        start = pl.multiple_of(m * 256, 256)
        rows = pl.ds(start, 256)
        sel = one_hot(col_ids[rows, :], lane_row)
        tile = gauss(block_points(start, 256), points[...], point_norms)
        ko[rows, :local] = (tile.astype(F32) + RIDGE * sel).astype(BF16)
        ko[rows, local:] = (-sel).astype(BF16)
        return carry

    lax.fori_loop(0, 4, left_operand, 0)

    def partial(which, j):
        lo_c, w = cols[j]
        rows = pl.ds(pl.multiple_of(which * half, half), half)
        cs = slice(lo_c, lo_c + w)
        return mm(ko[rows, :local], c_low[:, cs]) + mm(ko[rows, local:], targets[:, cs])

    def yrows(step):
        return pl.ds(pl.multiple_of(((y + step) % 4) * 128, 128), 128)

    swaps = []
    for j in range(n_chunks):
        b = bufs[j]
        b["p_send"][...] = partial(1 - core, j).astype(BF16)
        swaps.append({st: push(b["p_send"].at[yrows(st), :], b["p_recv"].at[yrows(st), :], partner)
                      for st in (2, 1, 3, 0)})

    reds = [dict() for _ in range(n_chunks)]

    def chip_sum(j, st, part=None):
        b = bufs[j]
        rows = yrows(st)
        return b["p_own"][rows, :] + b["p_recv"][rows, :].astype(F32)

    for j in range(n_chunks):
        b, r = bufs[j], reds[j]
        b["p_own"][...] = partial(core, j)
        swaps[j][2].wait_recv()
        b["far"][...] = chip_sum(j, 2).astype(BF16)
        r["fu"] = push(b["far"].at[0:64, :], b["rfar"].at[0], y_up)
        r["fd"] = push(b["far"].at[64:128, :], b["rfar"].at[1], y_dn)
        swaps[j][1].wait_recv()
        up = chip_sum(j, 1)
        b["near"][1] = up[64:].astype(BF16)
        r["nu"] = push(b["near"].at[1], b["rnear"].at[0, 1], y_up)
        swaps[j][3].wait_recv()
        dn = chip_sum(j, 3)
        b["near"][2] = dn[:64].astype(BF16)
        r["nd"] = push(b["near"].at[2], b["rnear"].at[1, 0], y_dn)
        b["p_own"][yrows(1), :] = up
        b["p_own"][yrows(3), :] = dn

    q0, q1 = block_points(0, half), block_points(half, half)
    same = one_hot(col_ids[half:, :], row_ids[:, :half])
    cross = (gauss(q1, q0, row_norms(q0)).astype(F32) + RIDGE * same).astype(BF16)
    hi, lo = split(inverses[0])
    hi, lo = split(mm(cross, hi) + mm(cross, lo))
    gb_hi[local:, :] = hi
    gb_lo[local:, :] = lo

    my_rows = pl.ds(pl.multiple_of(core * half + y * 128 + x * 64, 64), 64)
    x_rows = pl.ds(pl.multiple_of(core * half + y * 128 + (1 - x) * 64, 64), 64)

    def seg(j, rows):
        return bufs[j]["rbuf"].at[rows, :]

    def seg_rows(step, xx):
        return pl.ds(pl.multiple_of(core * half + ((y + step) % 4) * 128 + xx * 64, 64), 64)

    gats = [dict() for _ in range(n_chunks)]

    def stage_dep(j):
        b, r = bufs[j], reds[j]
        r["fu"].wait_recv()
        b["near"][0] = (b["p_own"][yrows(1), :][:64] + b["rfar"][0].astype(F32)).astype(BF16)
        r["du"] = push(b["near"].at[0], b["rnear"].at[0, 0], y_up)
        r["fd"].wait_recv()
        b["near"][3] = (b["p_own"][yrows(3), :][64:] + b["rfar"][1].astype(F32)).astype(BF16)
        r["dd"] = push(b["near"].at[3], b["rnear"].at[1, 1], y_dn)

    def stage_x(j):
        b, r = bufs[j], reds[j]
        swaps[j][0].wait_recv()
        for key in ("nu", "nd", "du", "dd"):
            r[key].wait_recv()

        def total(xx):
            rows = pl.ds(pl.multiple_of(y * 128 + xx * 64, 64), 64)
            return (b["p_own"][rows, :] + b["p_recv"][rows, :].astype(F32)
                    + b["rnear"][0, xx].astype(F32) + b["rnear"][1, xx].astype(F32))

        b["xs"][...] = total(1 - x).astype(BF16)
        r["x"] = push(b["xs"], b["xr"], x_nb)
        b["p_own"][pl.ds(pl.multiple_of(y * 128, 128), 64), :] = total(x)

    def stage_r(j):
        b, r, g = bufs[j], reds[j], gats[j]
        r["x"].wait_recv()
        mine = b["p_own"][pl.ds(pl.multiple_of(y * 128, 128), 64), :]
        b["rbuf"][my_rows, :] = (mine + b["xr"][...].astype(F32)).astype(BF16)
        g["x"] = push(seg(j, my_rows), seg(j, my_rows), x_nb)
        g["u0"] = push(seg(j, my_rows), seg(j, my_rows), y_up)
        g["d0"] = push(seg(j, my_rows), seg(j, my_rows), y_dn)
        g["share"] = [push(seg(j, my_rows), seg(j, my_rows), partner)]

    def pass_on(j, rows):
        gats[j]["share"].append(push(seg(j, rows), seg(j, rows), partner))

    def stage_y(j):
        g = gats[j]
        g["x"].wait_recv()
        g["u1"] = push(seg(j, x_rows), seg(j, x_rows), y_up)
        g["d1"] = push(seg(j, x_rows), seg(j, x_rows), y_dn)
        pass_on(j, x_rows)

    def stage_fwd(j):
        g = gats[j]
        g["u0"].wait_recv()
        below = seg_rows(3, x)
        g["fu"] = push(seg(j, below), seg(j, below), y_up)
        pass_on(j, below)
        g["d1"].wait_recv()
        above = seg_rows(1, 1 - x)
        g["fd"] = push(seg(j, above), seg(j, above), y_dn)
        pass_on(j, above)
        g["d0"].wait_recv()
        pass_on(j, seg_rows(1, x))
        g["u1"].wait_recv()
        pass_on(j, seg_rows(3, 1 - x))

    def stage_last(j):
        g = gats[j]
        g["fu"].wait_recv()
        pass_on(j, seg_rows(2, x))
        g["fd"].wait_recv()
        pass_on(j, seg_rows(2, 1 - x))

    stores = []

    def stage_out(j):
        b = bufs[j]
        lo_c, w = cols[j]
        for cp in gats[j]["share"]:
            cp.wait_recv()
        n0 = b["rbuf"][:half, :]
        both = mm(gb_hi[...], n0) + mm(gb_lo[...], n0)
        w_hi, w_lo = split(b["rbuf"][half:, :].astype(F32) - both[local:])
        upd = both[:local] + mm(g1_hi[...], w_hi) + mm(g1_hi[...], w_lo) + mm(g1_lo[...], w_hi)
        b["outv"][...] = coeffs[:, lo_c:lo_c + w] - upd
        st = pltpu.make_async_copy(b["outv"], out_hbm.at[:, lo_c:lo_c + w], store_sem.at[j])
        st.start()
        stores.append(st)

    stages = [stage_dep, stage_x, stage_r, stage_y, stage_fwd, stage_last, stage_out]
    for t in range(n_chunks + len(stages) - 1):
        for k, stage in enumerate(stages):
            if 0 <= t - k < n_chunks:
                stage(t - k)

    for st in stores:
        st.wait()
    for cp in sent:
        cp.wait_send()


def per_device(points, targets, coeffs, block_ids, inverses):
    local, feat = points.shape
    labels = targets.shape[1]
    block = block_ids.shape[1]
    n = 2 * block
    ids = block_ids.reshape(n)
    cols = []
    at = 0
    while at < labels:
        w = min(WIDE, labels - at)
        cols.append((at, w))
        at += w
    vm = pltpu.VMEM
    scratch = [
        vm((local, labels), BF16), vm((local, labels), F32), vm((2, block, block), F32),
        vm((local, labels), BF16), vm((n, 2 * local), BF16),
        vm((8, 64, LANES), BF16), vm((8, 64, LANES), BF16), vm((8, 64, LANES), BF16),
        vm((7, 64, LANES), BF16), vm((64, LANES), BF16), vm((8, n, LANES), BF16),
        vm((local + block, block), BF16), vm((local + block, block), BF16),
        vm((local, block), BF16), vm((local, block), BF16),
        pltpu.SemaphoreType.DMA((3,)), pltpu.SemaphoreType.DMA((len(cols),)),
        pltpu.SemaphoreType.DMA((COPIES,)), pltpu.SemaphoreType.DMA((COPIES,)),
    ]
    for _, w in cols:
        scratch += [
            vm((block, w), BF16), vm((block, w), F32), vm((block, w), BF16),
            vm((128, w), BF16), vm((2, 64, w), BF16), vm((4, 64, w), BF16), vm((2, 2, 64, w), BF16),
            vm((64, w), BF16), vm((64, w), BF16), vm((n, w), BF16), vm((local, w), F32),
        ]
    in_vmem = pl.BlockSpec(memory_space=pltpu.VMEM)
    in_any = pl.BlockSpec(memory_space=pl.ANY)
    return pl.pallas_call(
        functools.partial(body, tuple(cols)),
        out_shape=jax.ShapeDtypeStruct((local, labels), F32),
        in_specs=[in_vmem, in_vmem, in_vmem, in_any, in_any, in_any],
        out_specs=in_any,
        scratch_shapes=scratch,
        compiler_params=pltpu.CompilerParams(
            collective_id=0, has_side_effects=True, vmem_limit_bytes=60 << 20),
        name="descent",
    )(points, ids.reshape(n, 1), ids.reshape(1, n), targets, coeffs, inverses)


def solution(mesh):
    return jax.shard_map(
        per_device,
        mesh=mesh,
        in_specs=(P("rows", None), P("rows", "labels"), P("rows", "labels"), P(), P()),
        out_specs=P("rows", "labels"),
        check_vma=False,
    )
```

```python
import functools

import jax
import jax.numpy as jnp
from jax import lax
from jax.experimental import pallas as pl
from jax.experimental.pallas import tpu as pltpu
from jax.sharding import PartitionSpec as P

RIDGE = 0.5
MESH = pl.DeviceIdType.MESH
F32, BF16 = jnp.float32, jnp.bfloat16
LANES = 128
PARTS = ((0, 64), (64, 64), (128, 48))
SLAB = 176
COPIES = 176
NT = (((1,), (1,)), ((), ()))
TN = (((0,), (0,)), ((), ()))


def mm(a, b):
    return jnp.dot(a, b, preferred_element_type=F32)


def mm_nt(a, b):
    return lax.dot_general(a, b, NT, preferred_element_type=F32)


def split(x):
    hi = x.astype(BF16)
    return hi, (x - hi.astype(F32)).astype(BF16)


def one_hot(a, b):
    return jnp.where(a == b, 1.0, 0.0)


def row_norms(x):
    hi, lo = split(jnp.square(x.astype(F32)))
    ones = jnp.ones((8, x.shape[1]), BF16)
    return (mm_nt(ones, hi) + mm_nt(ones, lo))[0:1]


def gauss(left, right, right_norms):
    left_norms = jnp.sum(jnp.square(left.astype(F32)), axis=1, keepdims=True)
    dist = jnp.maximum(left_norms + right_norms - 2.0 * mm_nt(left, right), 0.0)
    return jnp.exp(-(2.0 / left.shape[1]) * dist).astype(BF16)


def body(points, ids, targets_hbm, coeffs_hbm, inverses_hbm, out_hbm, *scratch):
    (targets, coeffs, inverses, c_low, kt, sel, qm, qx_recv, qchip, qr_recv, qpiece, qbuf,
     weights, outv, load_sem, store_sem, send_sem, recv_sem) = scratch[:18]
    names = ("p_send", "p_own", "p_recv", "far", "rfar", "near", "rnear", "xs", "xr", "n_mine", "n_recv", "ubuf")
    bufs = [dict(zip(names, scratch[18 + len(names) * j: 18 + len(names) * (j + 1)])) for j in range(len(PARTS))]
    n_parts = len(PARTS)

    me = lax.axis_index("rows")
    lab = lax.axis_index("labels")
    core = me % 2
    chip = me // 2
    y = chip % 4
    x = chip // 4
    z = lab // 2
    xh = lab % 2
    block = ids.shape[1]
    local = points.shape[0]
    per_y = coeffs.shape[0] // 4

    def chip_peer(d):
        return {"rows": ((chip + d) % 8) * 2 + core}

    partner = {"rows": chip * 2 + 1 - core}
    y_up = {"rows": (x * 4 + (y + 1) % 4) * 2 + core}
    y_dn = {"rows": (x * 4 + (y + 3) % 4) * 2 + core}
    x_nb = {"rows": ((1 - x) * 4 + y) * 2 + core}
    z_up = {"labels": ((z + 1) % 8) * 2 + xh}
    z_dn = {"labels": ((z + 7) % 8) * 2 + xh}

    loads = [
        pltpu.make_async_copy(coeffs_hbm, coeffs, load_sem.at[0]),
        pltpu.make_async_copy(targets_hbm, targets, load_sem.at[1]),
        pltpu.make_async_copy(inverses_hbm, inverses, load_sem.at[2]),
    ]
    for ld in loads:
        ld.start()

    barrier = pltpu.get_barrier_semaphore()
    greet = [partner, z_up, z_dn] + [chip_peer(d) for d in range(1, 8)]
    for dev in greet:
        pl.semaphore_signal(barrier, inc=1, device_id=dev, device_id_type=MESH)

    sent = []

    def push(src, dst, dev):
        i = len(sent)
        cp = pltpu.make_async_remote_copy(
            src_ref=src, dst_ref=dst, send_sem=send_sem.at[i], recv_sem=recv_sem.at[i],
            device_id=dev, device_id_type=MESH)
        cp.start()
        sent.append(cp)
        return cp

    first_row = me * local
    sub_row = first_row + lax.broadcasted_iota(jnp.int32, (local, 1), 0)

    z_lanes = pl.ds(pl.multiple_of((z % 4) * 128, 128), 128)
    z_ids = jnp.where(z < 4, ids[0:1, z_lanes], ids[1:2, z_lanes])
    z_sel = one_hot(sub_row, z_ids).astype(BF16)
    found = lax.dot_general(z_sel, points[...], TN, preferred_element_type=F32).astype(BF16)
    for f in range(8):
        for h in range(2):
            qm[h, f] = found[h * 64:(h + 1) * 64, f * LANES:(f + 1) * LANES]
    pl.semaphore_wait(barrier, len(greet))
    qx = push(qm.at[1 - core], qx_recv, partner)
    for b in range(2):
        sel[b] = one_hot(sub_row, ids[b:b + 1, :]).astype(BF16)
    qx.wait_recv()
    qchip[...] = (qm[core].astype(F32) + qx_recv[...].astype(F32)).astype(BF16)
    red = [push(qchip.at[(chip + d) % 8], qr_recv.at[d - 1], chip_peer(d)) for d in range(1, 8)]

    piece = qchip[chip].astype(F32)
    for d in range(1, 8):
        red[d - 1].wait_recv()
        piece = piece + qr_recv[d - 1].astype(F32)
    qpiece[...] = piece.astype(BF16)
    zrows = pl.ds(pl.multiple_of(z * 128 + core * 64, 64), 64)
    qbuf[chip, zrows, :] = piece.astype(BF16)
    gat = [push(qpiece, qbuf.at[chip, zrows, :], chip_peer(d)) for d in range(1, 8)]
    for cp in gat:
        cp.wait_recv()

    def zchunk(zz, at, n):
        rows = pl.ds(pl.multiple_of((zz % 8) * 128 + core * 64, 64), 64)
        return qbuf.at[pl.ds(at, n), rows, :]

    shares = []

    def share_q(zz, at=0, n=8):
        shares.append(push(zchunk(zz, at, n), zchunk(zz, at, n), partner))

    hops = {}
    for s in range(1, 5):
        for h in range(4):
            for sign, dev in ((1, z_up), (-1, z_dn)):
                held = z + 8 - sign * (s - 1)
                if s > 1:
                    hops[sign, s - 1, h].wait_recv()
                if s < 4 or (h < 2) == (sign == 1):
                    hops[sign, s, h] = push(zchunk(held, 2 * h, 2), zchunk(held, 2 * h, 2), dev)
        share_q(z + 8 - (s - 1))
        if s > 1:
            share_q(z + 8 + (s - 1))
        if s == 1:
            loads[0].wait()
            c_low[...] = coeffs[...].astype(BF16)
    for sign, hs, at in ((1, (0, 1), 0), (-1, (2, 3), 4)):
        for h in hs:
            hops[sign, 4, h].wait_recv()
        share_q(z + 4, at, 4)
    for cp in shares:
        cp.wait_recv()

    def block_points(start, size):
        return jnp.concatenate([qbuf[f, pl.ds(start, size), :] for f in range(8)], axis=1)

    for b in range(2):
        q = block_points(b * block, block)
        tile = gauss(points[...], q, row_norms(q))
        kt[b] = (tile.astype(F32) + RIDGE * sel[b].astype(F32)).astype(BF16)

    loads[1].wait()

    def partial(b, st):
        rows = pl.ds(pl.multiple_of(((y + st) % 4) * per_y, 16), per_y)
        return mm(c_low[rows, :], kt[b]) - mm(targets[rows, :], sel[b])

    def put(name, st, value):
        for j, (at, h) in enumerate(PARTS):
            for xx in range(2):
                off = xx * (per_y - SLAB) + at
                ref = bufs[j][name]
                ref[pl.ds(((y + st) % 4) * 2 + xx, 1)] = value[off:off + h].astype(ref.dtype)[None]

    swaps = [dict() for _ in range(n_parts)]

    def send_half(st):
        put("p_send", st, partial(1 - core, st))
        at = pl.ds(((y + st) % 4) * 2, 2)
        for j in range(n_parts):
            swaps[j][st] = push(bufs[j]["p_send"].at[at], bufs[j]["p_recv"].at[at], partner)

    reds = [dict() for _ in range(n_parts)]

    def chip_sum(j, st, xx):
        s = ((y + st) % 4) * 2 + xx
        return bufs[j]["p_own"][s] + bufs[j]["p_recv"][s].astype(F32)

    send_half(2)
    put("p_own", 2, partial(core, 2))
    send_half(1)
    for j in range(n_parts):
        b, r = bufs[j], reds[j]
        swaps[j][2].wait_recv()
        for xx in range(2):
            b["far"][xx] = chip_sum(j, 2, xx).astype(BF16)
        r["fu"] = push(b["far"].at[0], b["rfar"].at[0], y_up)
        r["fd"] = push(b["far"].at[1], b["rfar"].at[1], y_dn)
    put("p_own", 1, partial(core, 1))
    send_half(3)
    put("p_own", 3, partial(core, 3))

    def stage_near(j):
        b, r = bufs[j], reds[j]
        swaps[j][1].wait_recv()
        b["near"][1] = chip_sum(j, 1, 1).astype(BF16)
        r["nu"] = push(b["near"].at[1], b["rnear"].at[0, 1], y_up)
        swaps[j][3].wait_recv()
        b["near"][2] = chip_sum(j, 3, 0).astype(BF16)
        r["nd"] = push(b["near"].at[2], b["rnear"].at[1, 0], y_dn)

    def stage_dep(j):
        b, r = bufs[j], reds[j]
        r["fu"].wait_recv()
        b["near"][0] = (chip_sum(j, 1, 0) + b["rfar"][0].astype(F32)).astype(BF16)
        r["du"] = push(b["near"].at[0], b["rnear"].at[0, 0], y_up)
        r["fd"].wait_recv()
        b["near"][3] = (chip_sum(j, 3, 1) + b["rfar"][1].astype(F32)).astype(BF16)
        r["dd"] = push(b["near"].at[3], b["rnear"].at[1, 1], y_dn)

    stage_near(0)
    send_half(0)
    put("p_own", 0, partial(core, 0))
    for j in range(n_parts):
        stage_dep(j)
        if j + 1 < n_parts:
            stage_near(j + 1)

    q0, q1 = block_points(0, block), block_points(block, block)
    eye = lax.broadcasted_iota(jnp.int32, (block, block), 0) == lax.broadcasted_iota(jnp.int32, (block, block), 1)
    ids0 = jnp.sum(jnp.where(eye, ids[0:1, :].astype(F32), 0.0), axis=1, keepdims=True)
    same = one_hot(ids0, ids[1:2, :].astype(F32))
    cross = (gauss(q0, q1, row_norms(q1)).astype(F32) + RIDGE * same).astype(BF16)
    loads[2].wait()
    hi, lo = split(inverses[0])
    b_hi, b_lo = split(mm(hi, cross) + mm(lo, cross))
    hi, lo = split(inverses[1])
    c_hi, c_lo = split(jnp.where(core == 1, mm(b_hi, hi) + mm(b_hi, lo) + mm(b_lo, hi), 0.0))
    weights[2] = c_hi
    weights[3] = c_lo
    hi, lo = split(inverses[core])
    weights[0] = hi
    weights[1] = lo

    def own(step, xx):
        return ((y + step) % 4) * 2 + xx

    def seg(j, s):
        return bufs[j]["ubuf"].at[core, s]

    gats = [dict() for _ in range(n_parts)]

    def stage_x(j):
        b, r = bufs[j], reds[j]
        swaps[j][0].wait_recv()
        for key in ("nu", "nd", "du", "dd"):
            r[key].wait_recv()

        def total(xx):
            return chip_sum(j, 0, xx) + b["rnear"][0, xx].astype(F32) + b["rnear"][1, xx].astype(F32)

        b["xs"][...] = total(1 - x).astype(BF16)
        r["x"] = push(b["xs"], b["xr"], x_nb)
        b["n_mine"][...] = total(x)

    def stage_swap(j):
        b, r = bufs[j], reds[j]
        r["x"].wait_recv()
        b["n_mine"][...] = b["n_mine"][...] + b["xr"][...].astype(F32)
        r["swap"] = push(b["n_mine"], b["n_recv"], partner)

    def times(n, w_hi, w_lo):
        hi, lo = split(n)
        return mm(hi, w_hi) + mm(lo, w_hi) + mm(hi, w_lo)

    def pass_on(j, s):
        gats[j]["share"].append(push(seg(j, s), seg(j, s), partner))

    def stage_u(j):
        b, r, g = bufs[j], reds[j], gats[j]
        mine = times(b["n_mine"][...], weights[0], weights[1])
        r["swap"].wait_recv()
        u = times(b["n_recv"][...], weights[2], weights[3]) - mine
        s = own(0, x)
        b["ubuf"][core, s] = u.astype(BF16)
        g["x"] = push(seg(j, s), seg(j, s), x_nb)
        g["u0"] = push(seg(j, s), seg(j, s), y_up)
        g["d0"] = push(seg(j, s), seg(j, s), y_dn)
        g["share"] = []
        pass_on(j, s)

    def stage_y(j):
        g = gats[j]
        g["x"].wait_recv()
        s = own(0, 1 - x)
        g["u1"] = push(seg(j, s), seg(j, s), y_up)
        g["d1"] = push(seg(j, s), seg(j, s), y_dn)
        pass_on(j, s)

    def stage_fwd(j):
        g = gats[j]
        g["u0"].wait_recv()
        below = own(3, x)
        g["fu"] = push(seg(j, below), seg(j, below), y_up)
        pass_on(j, below)
        g["d1"].wait_recv()
        above = own(1, 1 - x)
        g["fd"] = push(seg(j, above), seg(j, above), y_dn)
        pass_on(j, above)
        g["d0"].wait_recv()
        pass_on(j, own(1, x))
        g["u1"].wait_recv()
        pass_on(j, own(3, 1 - x))

    def stage_last(j):
        g = gats[j]
        g["fu"].wait_recv()
        pass_on(j, own(2, x))
        g["fd"].wait_recv()
        pass_on(j, own(2, 1 - x))

    stores = []

    def stage_out(j):
        ubuf = bufs[j]["ubuf"]
        at, h = PARTS[j]
        for cp in gats[j]["share"]:
            cp.wait_recv()
        upd = mm_nt(ubuf[0].reshape(8 * h, block), sel[0]) + mm_nt(ubuf[1].reshape(8 * h, block), sel[1])
        for s in range(8):
            skip = 2 * SLAB - per_y if at == 0 and s % 2 == 1 else 0
            first = (s // 2) * per_y + (s % 2) * (per_y - SLAB) + at + skip
            rows = slice(first, first + h - skip)
            outv[rows, :] = coeffs[rows, :] + upd[s * h + skip:(s + 1) * h]
            st = pltpu.make_async_copy(outv.at[rows, :], out_hbm.at[rows, :], store_sem.at[len(stores)])
            st.start()
            stores.append(st)

    stages = [stage_x, stage_swap, stage_u, stage_y, stage_fwd, stage_last, stage_out]
    for t in range(n_parts + len(stages) - 1):
        for k, stage in enumerate(stages):
            if 0 <= t - k < n_parts:
                stage(t - k)

    for st in stores:
        st.wait()
    for cp in sent:
        cp.wait_send()


def per_device(points, targets, coeffs, block_ids, inverses):
    local, feat = points.shape
    labels = targets.shape[1]
    block = block_ids.shape[1]
    n = 2 * block
    vm = pltpu.VMEM
    scratch = [
        vm((labels, local), BF16), vm((labels, local), F32), vm((2, block, block), F32),
        vm((labels, local), BF16), vm((2, local, block), BF16), vm((2, local, block), BF16),
        vm((2, 8, 64, LANES), BF16), vm((8, 64, LANES), BF16), vm((8, 64, LANES), BF16),
        vm((7, 64, LANES), BF16), vm((64, LANES), BF16), vm((8, n, LANES), BF16),
        vm((4, block, block), BF16), vm((labels, local), F32),
        pltpu.SemaphoreType.DMA((3,)), pltpu.SemaphoreType.DMA((8 * len(PARTS),)),
        pltpu.SemaphoreType.DMA((COPIES,)), pltpu.SemaphoreType.DMA((COPIES,)),
    ]
    for _, h in PARTS:
        scratch += [
            vm((8, h, block), BF16), vm((8, h, block), F32), vm((8, h, block), BF16),
            vm((2, h, block), BF16), vm((2, h, block), BF16), vm((4, h, block), BF16), vm((2, 2, h, block), BF16),
            vm((h, block), BF16), vm((h, block), BF16), vm((h, block), F32), vm((h, block), F32),
            vm((2, 8, h, block), BF16),
        ]
    in_vmem = pl.BlockSpec(memory_space=pltpu.VMEM)
    in_any = pl.BlockSpec(memory_space=pl.ANY)
    out = pl.pallas_call(
        body,
        out_shape=jax.ShapeDtypeStruct((labels, local), F32),
        in_specs=[in_vmem, in_vmem, in_any, in_any, in_any],
        out_specs=in_any,
        scratch_shapes=scratch,
        compiler_params=pltpu.CompilerParams(
            collective_id=0, has_side_effects=True, vmem_limit_bytes=60 << 20),
        name="descent",
    )(points, block_ids, targets.T, coeffs.T, inverses)
    return out.T


def solution(mesh):
    return jax.shard_map(
        per_device,
        mesh=mesh,
        in_specs=(P("rows", None), P("rows", "labels"), P("rows", "labels"), P(), P()),
        out_specs=P("rows", "labels"),
        check_vma=False,
    )
```

```python
import functools

import jax
import jax.numpy as jnp
from jax import lax
from jax.experimental import pallas as pl
from jax.experimental.pallas import tpu as pltpu
from jax.sharding import PartitionSpec as P

RIDGE = 0.5
MESH = pl.DeviceIdType.MESH
F32, BF16 = jnp.float32, jnp.bfloat16
LANES = 128
PARTS = ((0, 64), (64, 64), (128, 48))
SLAB = 176
COPIES = 176
NT = (((1,), (1,)), ((), ()))
TN = (((0,), (0,)), ((), ()))


def mm(a, b):
    return jnp.dot(a, b, preferred_element_type=F32)


def mm_nt(a, b):
    return lax.dot_general(a, b, NT, preferred_element_type=F32)


def split(x):
    hi = x.astype(BF16)
    return hi, (x - hi.astype(F32)).astype(BF16)


def one_hot(a, b):
    return jnp.where(a == b, 1.0, 0.0)


def row_norms(x):
    hi, lo = split(jnp.square(x.astype(F32)))
    ones = jnp.ones((8, x.shape[1]), BF16)
    return (mm_nt(ones, hi) + mm_nt(ones, lo))[0:1]


def col_norms(x):
    return jnp.sum(jnp.square(x.astype(F32)), axis=1, keepdims=True)


def gauss(left, left_norms, right, right_norms):
    dist = jnp.maximum(left_norms + right_norms - 2.0 * mm_nt(left, right), 0.0)
    return jnp.exp(-(2.0 / left.shape[1]) * dist).astype(BF16)


def body(points_hbm, ids_hbm, targets_hbm, coeffs_hbm, inverses_hbm, outv, *scratch):
    (points, ids, targets, coeffs, inverses, c_low, kt, sel, qm, qx_recv, qchip, qr_recv, qpiece, qbuf,
     weights, point_norms, load_sem, send_sem, recv_sem) = scratch[:19]
    names = ("p_send", "p_own", "p_recv", "far", "rfar", "near", "rnear", "xs", "xr", "n_mine", "n_recv", "ubuf")
    bufs = [dict(zip(names, scratch[19 + len(names) * j: 19 + len(names) * (j + 1)])) for j in range(len(PARTS))]
    n_parts = len(PARTS)

    me = lax.axis_index("rows")
    lab = lax.axis_index("labels")
    core = me % 2
    chip = me // 2
    y = chip % 4
    x = chip // 4
    z = lab // 2
    xh = lab % 2
    block = ids_hbm.shape[1]
    local = points.shape[0]
    per_y = coeffs.shape[0] // 4

    def chip_peer(d):
        return {"rows": ((chip + d) % 8) * 2 + core}

    partner = {"rows": chip * 2 + 1 - core}
    y_up = {"rows": (x * 4 + (y + 1) % 4) * 2 + core}
    y_dn = {"rows": (x * 4 + (y + 3) % 4) * 2 + core}
    x_nb = {"rows": ((1 - x) * 4 + y) * 2 + core}
    z_up = {"labels": ((z + 1) % 8) * 2 + xh}
    z_dn = {"labels": ((z + 7) % 8) * 2 + xh}

    loads = [
        pltpu.make_async_copy(coeffs_hbm, coeffs, load_sem.at[0]),
        pltpu.make_async_copy(targets_hbm, targets, load_sem.at[1]),
        pltpu.make_async_copy(inverses_hbm, inverses, load_sem.at[2]),
        pltpu.make_async_copy(points_hbm, points, load_sem.at[3]),
        pltpu.make_async_copy(ids_hbm, ids, load_sem.at[4]),
    ]
    for ld in loads[::-1]:
        ld.start()

    barrier = pltpu.get_barrier_semaphore()
    greet = [partner, z_up, z_dn] + [chip_peer(d) for d in range(1, 8)]
    for dev in greet:
        pl.semaphore_signal(barrier, inc=1, device_id=dev, device_id_type=MESH)

    sent = []

    def push(src, dst, dev):
        i = len(sent)
        cp = pltpu.make_async_remote_copy(
            src_ref=src, dst_ref=dst, send_sem=send_sem.at[i], recv_sem=recv_sem.at[i],
            device_id=dev, device_id_type=MESH)
        cp.start()
        sent.append(cp)
        return cp

    first_row = me * local
    sub_row = first_row + lax.broadcasted_iota(jnp.int32, (local, 1), 0)

    loads[4].wait()
    loads[3].wait()
    z_lanes = pl.ds(pl.multiple_of((z % 4) * 128, 128), 128)
    z_ids = jnp.where(z < 4, ids[0:1, z_lanes], ids[1:2, z_lanes])
    z_sel = one_hot(sub_row, z_ids).astype(BF16)
    found = lax.dot_general(z_sel, points[...], TN, preferred_element_type=F32).astype(BF16)
    for f in range(8):
        for h in range(2):
            qm[h, f] = found[h * 64:(h + 1) * 64, f * LANES:(f + 1) * LANES]
    pl.semaphore_wait(barrier, len(greet))
    qx = push(qm.at[1 - core], qx_recv, partner)
    for b in range(2):
        sel[b] = one_hot(sub_row, ids[b:b + 1, :]).astype(BF16)
    qx.wait_recv()
    qchip[...] = (qm[core].astype(F32) + qx_recv[...].astype(F32)).astype(BF16)
    red = [push(qchip.at[(chip + d) % 8], qr_recv.at[d - 1], chip_peer(d)) for d in range(1, 8)]

    piece = qchip[chip].astype(F32)
    for d in range(1, 8):
        red[d - 1].wait_recv()
        piece = piece + qr_recv[d - 1].astype(F32)
    qpiece[...] = piece.astype(BF16)
    zrows = pl.ds(pl.multiple_of(z * 128 + core * 64, 64), 64)
    qbuf[chip, zrows, :] = piece.astype(BF16)
    gat = [push(qpiece, qbuf.at[chip, zrows, :], chip_peer(d)) for d in range(1, 8)]
    for cp in gat:
        cp.wait_recv()

    def zchunk(zz, at, n):
        rows = pl.ds(pl.multiple_of((zz % 8) * 128 + core * 64, 64), 64)
        return qbuf.at[pl.ds(at, n), rows, :]

    shares = []

    def share_q(zz, at=0, n=8):
        shares.append(push(zchunk(zz, at, n), zchunk(zz, at, n), partner))

    def block_points(start, size):
        return jnp.concatenate([qbuf[f, pl.ds(start, size), :] for f in range(8)], axis=1)

    def fill_tile(zz, *arrived):
        for i in arrived:
            shares[i].wait_recv()
        zz = zz % 8
        lanes = pl.ds(pl.multiple_of((zz % 4) * 128, 128), 128)
        q = block_points(pl.multiple_of(zz * 128, 128), 128)
        tile = gauss(points[...], point_norms[...], q, row_norms(q))
        pick = sel[zz // 4, :, lanes].astype(F32)
        kt[zz // 4, :, lanes] = (tile.astype(F32) + RIDGE * pick).astype(BF16)

    hops = {}
    for s in range(1, 5):
        for h in range(4):
            for sign, dev in ((1, z_up), (-1, z_dn)):
                held = z + 8 - sign * (s - 1)
                if s > 1:
                    hops[sign, s - 1, h].wait_recv()
                if s < 4 or (h < 2) == (sign == 1):
                    hops[sign, s, h] = push(zchunk(held, 2 * h, 2), zchunk(held, 2 * h, 2), dev)
        share_q(z + 8 - (s - 1))
        if s > 1:
            share_q(z + 8 + (s - 1))
        if s == 1:
            loads[0].wait()
            c_low[...] = coeffs[...].astype(BF16)
            point_norms[...] = col_norms(points[...])
        elif s == 2:
            fill_tile(z, 0)
        elif s == 3:
            fill_tile(z + 7, 1)
            fill_tile(z + 1, 2)
        else:
            fill_tile(z + 6, 3)
            fill_tile(z + 2, 4)
    for sign, hs, at in ((1, (0, 1), 0), (-1, (2, 3), 4)):
        for h in hs:
            hops[sign, 4, h].wait_recv()
        share_q(z + 4, at, 4)
    fill_tile(z + 5, 5)
    fill_tile(z + 3, 6)
    fill_tile(z + 4, 7, 8)

    loads[1].wait()

    def partial(b, st):
        rows = pl.ds(pl.multiple_of(((y + st) % 4) * per_y, 16), per_y)
        return mm(c_low[rows, :], kt[b]) - mm(targets[rows, :], sel[b])

    def put(name, st, value):
        for j, (at, h) in enumerate(PARTS):
            for xx in range(2):
                off = xx * (per_y - SLAB) + at
                ref = bufs[j][name]
                ref[pl.ds(((y + st) % 4) * 2 + xx, 1)] = value[off:off + h].astype(ref.dtype)[None]

    swaps = [dict() for _ in range(n_parts)]

    def send_half(st):
        put("p_send", st, partial(1 - core, st))
        at = pl.ds(((y + st) % 4) * 2, 2)
        for j in range(n_parts):
            swaps[j][st] = push(bufs[j]["p_send"].at[at], bufs[j]["p_recv"].at[at], partner)

    reds = [dict() for _ in range(n_parts)]

    def chip_sum(j, st, xx):
        s = ((y + st) % 4) * 2 + xx
        return bufs[j]["p_own"][s] + bufs[j]["p_recv"][s].astype(F32)

    send_half(2)
    put("p_own", 2, partial(core, 2))
    send_half(1)
    for j in range(n_parts):
        b, r = bufs[j], reds[j]
        swaps[j][2].wait_recv()
        for xx in range(2):
            b["far"][xx] = chip_sum(j, 2, xx).astype(BF16)
        r["fu"] = push(b["far"].at[0], b["rfar"].at[0], y_up)
        r["fd"] = push(b["far"].at[1], b["rfar"].at[1], y_dn)
    put("p_own", 1, partial(core, 1))
    send_half(3)
    put("p_own", 3, partial(core, 3))

    def stage_near(j):
        b, r = bufs[j], reds[j]
        swaps[j][1].wait_recv()
        b["near"][1] = chip_sum(j, 1, 1).astype(BF16)
        r["nu"] = push(b["near"].at[1], b["rnear"].at[0, 1], y_up)
        swaps[j][3].wait_recv()
        b["near"][2] = chip_sum(j, 3, 0).astype(BF16)
        r["nd"] = push(b["near"].at[2], b["rnear"].at[1, 0], y_dn)

    def stage_dep(j):
        b, r = bufs[j], reds[j]
        r["fu"].wait_recv()
        b["near"][0] = (chip_sum(j, 1, 0) + b["rfar"][0].astype(F32)).astype(BF16)
        r["du"] = push(b["near"].at[0], b["rnear"].at[0, 0], y_up)
        r["fd"].wait_recv()
        b["near"][3] = (chip_sum(j, 3, 1) + b["rfar"][1].astype(F32)).astype(BF16)
        r["dd"] = push(b["near"].at[3], b["rnear"].at[1, 1], y_dn)

    stage_near(0)
    send_half(0)
    put("p_own", 0, partial(core, 0))
    for j in range(n_parts):
        stage_dep(j)
        if j + 1 < n_parts:
            stage_near(j + 1)

    q0, q1 = block_points(0, block), block_points(block, block)
    eye = lax.broadcasted_iota(jnp.int32, (block, block), 0) == lax.broadcasted_iota(jnp.int32, (block, block), 1)
    ids0 = jnp.sum(jnp.where(eye, ids[0:1, :].astype(F32), 0.0), axis=1, keepdims=True)
    same = one_hot(ids0, ids[1:2, :].astype(F32))
    cross = (gauss(q0, col_norms(q0), q1, row_norms(q1)).astype(F32) + RIDGE * same).astype(BF16)
    loads[2].wait()
    hi, lo = split(inverses[0])
    b_hi, b_lo = split(mm(hi, cross) + mm(lo, cross))
    hi, lo = split(inverses[1])
    c_hi, c_lo = split(jnp.where(core == 1, mm(b_hi, hi) + mm(b_hi, lo) + mm(b_lo, hi), 0.0))
    weights[2] = c_hi
    weights[3] = c_lo
    hi, lo = split(inverses[core])
    weights[0] = hi
    weights[1] = lo

    def own(step, xx):
        return ((y + step) % 4) * 2 + xx

    def seg(j, s):
        return bufs[j]["ubuf"].at[core, s]

    gats = [dict() for _ in range(n_parts)]

    def stage_x(j):
        b, r = bufs[j], reds[j]
        swaps[j][0].wait_recv()
        for key in ("nu", "nd", "du", "dd"):
            r[key].wait_recv()

        def total(xx):
            return chip_sum(j, 0, xx) + b["rnear"][0, xx].astype(F32) + b["rnear"][1, xx].astype(F32)

        b["xs"][...] = total(1 - x).astype(BF16)
        r["x"] = push(b["xs"], b["xr"], x_nb)
        b["n_mine"][...] = total(x)

    def stage_swap(j):
        b, r = bufs[j], reds[j]
        r["x"].wait_recv()
        b["n_mine"][...] = b["n_mine"][...] + b["xr"][...].astype(F32)
        r["swap"] = push(b["n_mine"], b["n_recv"], partner)

    def times(n, w_hi, w_lo):
        hi, lo = split(n)
        return mm(hi, w_hi) + mm(lo, w_hi) + mm(hi, w_lo)

    def pass_on(j, s):
        gats[j]["share"].append(push(seg(j, s), seg(j, s), partner))

    def stage_u(j):
        b, r, g = bufs[j], reds[j], gats[j]
        mine = times(b["n_mine"][...], weights[0], weights[1])
        r["swap"].wait_recv()
        u = times(b["n_recv"][...], weights[2], weights[3]) - mine
        s = own(0, x)
        b["ubuf"][core, s] = u.astype(BF16)
        g["x"] = push(seg(j, s), seg(j, s), x_nb)
        g["u0"] = push(seg(j, s), seg(j, s), y_up)
        g["d0"] = push(seg(j, s), seg(j, s), y_dn)
        g["share"] = []
        pass_on(j, s)

    def stage_y(j):
        g = gats[j]
        g["x"].wait_recv()
        s = own(0, 1 - x)
        g["u1"] = push(seg(j, s), seg(j, s), y_up)
        g["d1"] = push(seg(j, s), seg(j, s), y_dn)
        pass_on(j, s)

    def stage_fwd(j):
        g = gats[j]
        g["u0"].wait_recv()
        below = own(3, x)
        g["fu"] = push(seg(j, below), seg(j, below), y_up)
        pass_on(j, below)
        g["d1"].wait_recv()
        above = own(1, 1 - x)
        g["fd"] = push(seg(j, above), seg(j, above), y_dn)
        pass_on(j, above)
        g["d0"].wait_recv()
        pass_on(j, own(1, x))
        g["u1"].wait_recv()
        pass_on(j, own(3, 1 - x))

    def stage_last(j):
        g = gats[j]
        g["fu"].wait_recv()
        pass_on(j, own(2, x))
        g["fd"].wait_recv()
        pass_on(j, own(2, 1 - x))

    def stage_out(j):
        ubuf = bufs[j]["ubuf"]
        at, h = PARTS[j]
        for cp in gats[j]["share"]:
            cp.wait_recv()
        upd = mm_nt(ubuf[0].reshape(8 * h, block), sel[0]) + mm_nt(ubuf[1].reshape(8 * h, block), sel[1])
        for s in range(8):
            skip = 2 * SLAB - per_y if at == 0 and s % 2 == 1 else 0
            first = (s // 2) * per_y + (s % 2) * (per_y - SLAB) + at + skip
            rows = slice(first, first + h - skip)
            outv[rows, :] = coeffs[rows, :] + upd[s * h + skip:(s + 1) * h]

    stages = [stage_x, stage_swap, stage_u, stage_y, stage_fwd, stage_last, stage_out]
    for t in range(n_parts + len(stages) - 1):
        for k, stage in enumerate(stages):
            if 0 <= t - k < n_parts:
                stage(t - k)

    for cp in sent:
        cp.wait_send()


def per_device(points, targets, coeffs, block_ids, inverses):
    local, feat = points.shape
    labels = targets.shape[1]
    block = block_ids.shape[1]
    n = 2 * block
    vm = pltpu.VMEM
    scratch = [
        vm((local, feat), BF16), vm((2, block), jnp.int32), vm((labels, local), BF16), vm((labels, local), F32), vm((2, block, block), F32),
        vm((labels, local), BF16), vm((2, local, block), BF16), vm((2, local, block), BF16),
        vm((2, 8, 64, LANES), BF16), vm((8, 64, LANES), BF16), vm((8, 64, LANES), BF16),
        vm((7, 64, LANES), BF16), vm((64, LANES), BF16), vm((8, n, LANES), BF16),
        vm((4, block, block), BF16), vm((local, 1), F32),
        pltpu.SemaphoreType.DMA((5,)),
        pltpu.SemaphoreType.DMA((COPIES,)), pltpu.SemaphoreType.DMA((COPIES,)),
    ]
    for _, h in PARTS:
        scratch += [
            vm((8, h, block), BF16), vm((8, h, block), F32), vm((8, h, block), BF16),
            vm((2, h, block), BF16), vm((2, h, block), BF16), vm((4, h, block), BF16), vm((2, 2, h, block), BF16),
            vm((h, block), BF16), vm((h, block), BF16), vm((h, block), F32), vm((h, block), F32),
            vm((2, 8, h, block), BF16),
        ]
    in_vmem = pl.BlockSpec(memory_space=pltpu.VMEM)
    in_any = pl.BlockSpec(memory_space=pltpu.HBM)
    out = pl.pallas_call(
        body,
        out_shape=jax.ShapeDtypeStruct((labels, local), F32),
        in_specs=[in_any] * 5,
        out_specs=in_vmem,
        scratch_shapes=scratch,
        compiler_params=pltpu.CompilerParams(
            collective_id=0, has_side_effects=True, vmem_limit_bytes=44 << 20),
        name="descent",
    )(*[pltpu.with_memory_space_constraint(a, pltpu.HBM)
        for a in (points, block_ids, targets.T, coeffs.T, inverses)])
    return out.T


def solution(mesh):
    return jax.shard_map(
        per_device,
        mesh=mesh,
        in_specs=(P("rows", None), P("rows", "labels"), P("rows", "labels"), P(), P()),
        out_specs=P("rows", "labels"),
        check_vma=False,
    )
```

```python
import functools

import jax
import jax.numpy as jnp
from jax import lax
from jax.experimental import pallas as pl
from jax.experimental.pallas import tpu as pltpu
from jax.sharding import PartitionSpec as P

RIDGE = 0.5
MESH = pl.DeviceIdType.MESH
F32, BF16 = jnp.float32, jnp.bfloat16
LANES = 128
PARTS = ((0, 64, False), (64, 64, True), (128, 48, False))
SLAB = 176
COPIES = 176
NT = (((1,), (1,)), ((), ()))
TN = (((0,), (0,)), ((), ()))


def mm(a, b):
    return jnp.dot(a, b, preferred_element_type=F32)


def mm_nt(a, b):
    return lax.dot_general(a, b, NT, preferred_element_type=F32)


def split(x):
    hi = x.astype(BF16)
    return hi, (x - hi.astype(F32)).astype(BF16)


def one_hot(a, b):
    return jnp.where(a == b, 1.0, 0.0)


def row_norms(x):
    hi, lo = split(jnp.square(x.astype(F32)))
    ones = jnp.ones((8, x.shape[1]), BF16)
    return (mm_nt(ones, hi) + mm_nt(ones, lo))[0:1]


def col_norms(x):
    return jnp.sum(jnp.square(x.astype(F32)), axis=1, keepdims=True)


def gauss(left, left_norms, right, right_norms):
    dist = jnp.maximum(left_norms + right_norms - 2.0 * mm_nt(left, right), 0.0)
    return jnp.exp(-(2.0 / left.shape[1]) * dist).astype(BF16)


def body(points_hbm, ids_hbm, targets_hbm, coeffs_hbm, inverses_hbm, outv, *scratch):
    (points, ids, targets, coeffs, inverses, c_low, kt, sel, qm, qx_recv, qchip, qr_recv, qpiece, qbuf,
     weights, point_norms, load_sem, send_sem, recv_sem) = scratch[:19]
    names = ("p_send", "p_own", "p_recv", "far", "rfar", "near", "rnear", "xs", "xr", "xsum", "n_mine", "n_recv", "ubuf")
    bufs = [dict(zip(names, scratch[19 + len(names) * j: 19 + len(names) * (j + 1)])) for j in range(len(PARTS))]
    n_parts = len(PARTS)

    me = lax.axis_index("rows")
    lab = lax.axis_index("labels")
    core = me % 2
    chip = me // 2
    y = chip % 4
    x = chip // 4
    z = lab // 2
    xh = lab % 2
    block = ids_hbm.shape[1]
    local = points.shape[0]
    per_y = coeffs.shape[0] // 4

    def chip_peer(d):
        return {"rows": ((chip + d) % 8) * 2 + core}

    partner = {"rows": chip * 2 + 1 - core}
    y_up = {"rows": (x * 4 + (y + 1) % 4) * 2 + core}
    y_dn = {"rows": (x * 4 + (y + 3) % 4) * 2 + core}
    x_nb = {"rows": ((1 - x) * 4 + y) * 2 + core}
    z_up = {"labels": ((z + 1) % 8) * 2 + xh}
    z_dn = {"labels": ((z + 7) % 8) * 2 + xh}

    loads = [
        pltpu.make_async_copy(coeffs_hbm, coeffs, load_sem.at[0]),
        pltpu.make_async_copy(targets_hbm, targets, load_sem.at[1]),
        pltpu.make_async_copy(inverses_hbm, inverses, load_sem.at[2]),
        pltpu.make_async_copy(points_hbm, points, load_sem.at[3]),
        pltpu.make_async_copy(ids_hbm, ids, load_sem.at[4]),
    ]
    for ld in loads[::-1]:
        ld.start()

    barrier = pltpu.get_barrier_semaphore()
    greet = [partner, z_up, z_dn] + [chip_peer(d) for d in range(1, 8)]
    for dev in greet:
        pl.semaphore_signal(barrier, inc=1, device_id=dev, device_id_type=MESH)

    sent = []

    def push(src, dst, dev):
        i = len(sent)
        cp = pltpu.make_async_remote_copy(
            src_ref=src, dst_ref=dst, send_sem=send_sem.at[i], recv_sem=recv_sem.at[i],
            device_id=dev, device_id_type=MESH)
        cp.start()
        sent.append(cp)
        return cp

    first_row = me * local
    sub_row = first_row + lax.broadcasted_iota(jnp.int32, (local, 1), 0)

    loads[4].wait()
    loads[3].wait()
    z_lanes = pl.ds(pl.multiple_of((z % 4) * 128, 128), 128)
    z_ids = jnp.where(z < 4, ids[0:1, z_lanes], ids[1:2, z_lanes])
    z_sel = one_hot(sub_row, z_ids).astype(BF16)
    found = lax.dot_general(z_sel, points[...], TN, preferred_element_type=F32).astype(BF16)
    for f in range(8):
        for h in range(2):
            qm[h, f] = found[h * 64:(h + 1) * 64, f * LANES:(f + 1) * LANES]
    pl.semaphore_wait(barrier, len(greet))
    qx = push(qm.at[1 - core], qx_recv, partner)
    for b in range(2):
        sel[b] = one_hot(sub_row, ids[b:b + 1, :]).astype(BF16)
    qx.wait_recv()
    qchip[...] = (qm[core].astype(F32) + qx_recv[...].astype(F32)).astype(BF16)
    par = y % 2

    def group(c):
        return (c % 2) * 4 + (c % 4 // 2) * 2 + c // 4

    red = [push(qchip.at[group((chip + d) % 8)], qr_recv.at[d - 1], chip_peer(d)) for d in range(1, 8)]

    mine = group(chip)
    piece = qchip[mine].astype(F32)
    for d in range(1, 8):
        red[d - 1].wait_recv()
        piece = piece + qr_recv[d - 1].astype(F32)
    qpiece[...] = piece.astype(BF16)
    zrows = pl.ds(pl.multiple_of(z * 128 + core * 64, 64), 64)
    qbuf[mine, zrows, :] = piece.astype(BF16)
    gat = [push(qpiece, qbuf.at[mine, zrows, :], dev) for dev in
           (x_nb, {"rows": (x * 4 + (y + 2) % 4) * 2 + core}, {"rows": ((1 - x) * 4 + (y + 2) % 4) * 2 + core})]
    for cp in gat:
        cp.wait_recv()

    def zchunk(zz, at, n):
        rows = pl.ds(pl.multiple_of((zz % 8) * 128 + core * 64, 64), 64)
        return qbuf.at[pl.ds(at, n), rows, :]

    def block_points(start, size):
        return jnp.concatenate([qbuf[f, pl.ds(start, size), :] for f in range(8)], axis=1)

    def fill_tile(zz):
        zz = zz % 8
        lanes = pl.ds(pl.multiple_of((zz % 4) * 128, 128), 128)
        q = block_points(pl.multiple_of(zz * 128, 128), 128)
        tile = gauss(points[...], point_norms[...], q, row_norms(q))
        pick = sel[zz // 4, :, lanes].astype(F32)
        kt[zz // 4, :, lanes] = (tile.astype(F32) + RIDGE * pick).astype(BF16)

    shared = {}

    def share_groups(k, which):
        held = zchunk(z + 8 + k, 4 * which, 4)
        return push(held, held, partner)

    aside = {}

    def y_push(k, h):
        held = zchunk(z + 8 + k, 4 * par + 2 * h, 2)
        aside[k, h] = push(held, held, y_up if h == 0 else y_dn)

    def close(k):
        for h in range(2):
            aside[k, h].wait_recv()
        shared[k] = shared[k] + [share_groups(k, 1 - par)]

    def fill(k):
        for cp in shared[k]:
            cp.wait_recv()
        fill_tile(z + 8 + k)

    hops = {}
    for s in range(1, 5):
        for h in range(2):
            for sign, dev in ((1, z_up), (-1, z_dn)):
                k = -sign * (s - 1)
                if s > 1:
                    hops[sign, s - 1, h].wait_recv()
                if s < 4 or (h == 0) == (sign == 1):
                    held = zchunk(z + 8 + k, 4 * par + 2 * h, 2)
                    hops[sign, s, h] = push(held, held, dev)
                if s > 1 or sign == 1:
                    y_push(k, h)
        for k in sorted({1 - s, s - 1}):
            shared[k] = [share_groups(k, par)]
        if s == 1:
            point_norms[...] = col_norms(points[...])
            loads[0].wait()
            c_low[...] = coeffs[...].astype(BF16)
        elif s == 2:
            close(0)
        elif s == 3:
            fill(0)
            close(-1)
            close(1)
        else:
            fill(-1)
            fill(1)
            close(-2)
            close(2)
    hops[1, 4, 0].wait_recv()
    y_push(4, 0)
    hops[-1, 4, 1].wait_recv()
    y_push(4, 1)
    shared[4] = [share_groups(4, par)]
    close(-3)
    close(3)
    fill(-2)
    fill(2)
    close(4)
    fill(-3)
    fill(3)
    fill(4)

    loads[1].wait()

    def partial(b, st):
        rows = pl.ds(pl.multiple_of(((y + st) % 4) * per_y, 16), per_y)
        return mm(c_low[rows, :], kt[b]) - mm(targets[rows, :], sel[b])

    def put(name, st, value):
        for j, (at, h, _) in enumerate(PARTS):
            for xx in range(2):
                off = xx * (per_y - SLAB) + at
                ref = bufs[j][name]
                ref[pl.ds(((y + st) % 4) * 2 + xx, 1)] = value[off:off + h].astype(ref.dtype)[None]

    swaps = [dict() for _ in range(n_parts)]

    def send_half(st):
        put("p_send", st, partial(1 - core, st))
        at = pl.ds(((y + st) % 4) * 2, 2)
        for j in range(n_parts):
            swaps[j][st] = push(bufs[j]["p_send"].at[at], bufs[j]["p_recv"].at[at], partner)

    reds = [dict() for _ in range(n_parts)]

    def chip_sum(j, st, xx):
        s = ((y + st) % 4) * 2 + xx
        return bufs[j]["p_own"][s] + bufs[j]["p_recv"][s].astype(F32)

    x_first = [mode for _, _, mode in PARTS]
    mid = block // 2

    def stage_cross(j, st):
        b, r = bufs[j], reds[j]
        if x_first[j]:
            swaps[j][st].wait_recv()
            b["xs"][st] = chip_sum(j, st, 1 - x).astype(BF16)
            r["x", st] = push(b["xs"].at[st], b["xr"].at[st], x_nb)

    def join(j, st):
        b = bufs[j]
        if x_first[j]:
            reds[j]["x", st].wait_recv()
            b["xsum"][st] = chip_sum(j, st, x) + b["xr"][st].astype(F32)
        else:
            swaps[j][st].wait_recv()

    def val(j, st, half):
        if x_first[j]:
            return bufs[j]["xsum"][st, :, half * mid:(half + 1) * mid]
        return chip_sum(j, st, half)

    def stage_far(j):
        b, r = bufs[j], reds[j]
        join(j, 2)
        for half in range(2):
            b["far"][half] = val(j, 2, half).astype(BF16)
        r["fu"] = push(b["far"].at[0], b["rfar"].at[0], y_up)
        r["fd"] = push(b["far"].at[1], b["rfar"].at[1], y_dn)

    def stage_near(j):
        b, r = bufs[j], reds[j]
        join(j, 1)
        b["near"][1] = val(j, 1, 1).astype(BF16)
        r["nu"] = push(b["near"].at[1], b["rnear"].at[0, 1], y_up)
        join(j, 3)
        b["near"][2] = val(j, 3, 0).astype(BF16)
        r["nd"] = push(b["near"].at[2], b["rnear"].at[1, 0], y_dn)

    def stage_dep(j):
        b, r = bufs[j], reds[j]
        r["fu"].wait_recv()
        b["near"][0] = (val(j, 1, 0) + b["rfar"][0].astype(F32)).astype(BF16)
        r["du"] = push(b["near"].at[0], b["rnear"].at[0, 0], y_up)
        r["fd"].wait_recv()
        b["near"][3] = (val(j, 3, 1) + b["rfar"][1].astype(F32)).astype(BF16)
        r["dd"] = push(b["near"].at[3], b["rnear"].at[1, 1], y_dn)

    y_parts = [j for j in range(n_parts) if not x_first[j]]
    x_parts = [j for j in range(n_parts) if x_first[j]]

    send_half(2)
    put("p_own", 2, partial(core, 2))
    send_half(1)
    for j in x_parts:
        stage_cross(j, 2)
    for j in y_parts:
        stage_far(j)
    put("p_own", 1, partial(core, 1))
    for j in x_parts:
        stage_cross(j, 1)
    send_half(3)
    put("p_own", 3, partial(core, 3))
    stage_near(y_parts[0])
    for j in x_parts:
        stage_cross(j, 3)
    send_half(0)
    put("p_own", 0, partial(core, 0))
    stage_dep(y_parts[0])
    for j in x_parts:
        stage_cross(j, 0)
        stage_far(j)
        stage_near(j)
    for j in y_parts[1:]:
        stage_near(j)
    for j in x_parts + y_parts[1:]:
        stage_dep(j)

    q0, q1 = block_points(0, block), block_points(block, block)
    eye = lax.broadcasted_iota(jnp.int32, (block, block), 0) == lax.broadcasted_iota(jnp.int32, (block, block), 1)
    ids0 = jnp.sum(jnp.where(eye, ids[0:1, :].astype(F32), 0.0), axis=1, keepdims=True)
    same = one_hot(ids0, ids[1:2, :].astype(F32))
    cross = (gauss(q0, col_norms(q0), q1, row_norms(q1)).astype(F32) + RIDGE * same).astype(BF16)
    loads[2].wait()
    hi, lo = split(inverses[0])
    b_hi, b_lo = split(mm(hi, cross) + mm(lo, cross))
    hi, lo = split(inverses[1])
    c_hi, c_lo = split(jnp.where(core == 1, mm(b_hi, hi) + mm(b_hi, lo) + mm(b_lo, hi), 0.0))
    weights[2] = c_hi
    weights[3] = c_lo
    hi, lo = split(inverses[core])
    weights[0] = hi
    weights[1] = lo

    def own(step, xx):
        return ((y + step) % 4) * 2 + xx

    def seg(j, s):
        return bufs[j]["ubuf"].at[core, s]

    gats = [dict() for _ in range(n_parts)]

    def stage_x(j):
        b, r = bufs[j], reds[j]
        join(j, 0)
        for key in ("nu", "nd", "du", "dd"):
            r[key].wait_recv()

        def total(half):
            return val(j, 0, half) + b["rnear"][0, half].astype(F32) + b["rnear"][1, half].astype(F32)

        if x_first[j]:
            b["n_mine"][:, :mid] = total(0)
            b["n_mine"][:, mid:] = total(1)
        else:
            b["xs"][...] = total(1 - x).astype(BF16)
            r["x"] = push(b["xs"], b["xr"], x_nb)
            b["n_mine"][...] = total(x)

    def stage_swap(j):
        b, r = bufs[j], reds[j]
        if not x_first[j]:
            r["x"].wait_recv()
            b["n_mine"][...] = b["n_mine"][...] + b["xr"][...].astype(F32)
        r["swap"] = push(b["n_mine"], b["n_recv"], partner)

    def times(n, w_hi, w_lo):
        hi, lo = split(n)
        return mm(hi, w_hi) + mm(lo, w_hi) + mm(hi, w_lo)

    def pass_on(j, s):
        gats[j]["share"].append(push(seg(j, s), seg(j, s), partner))

    def stage_u(j):
        b, r, g = bufs[j], reds[j], gats[j]
        mine = times(b["n_mine"][...], weights[0], weights[1])
        r["swap"].wait_recv()
        u = times(b["n_recv"][...], weights[2], weights[3]) - mine
        s = own(0, x)
        b["ubuf"][core, s] = u.astype(BF16)
        g["x"] = push(seg(j, s), seg(j, s), x_nb)
        g["u0"] = push(seg(j, s), seg(j, s), y_up)
        g["d0"] = push(seg(j, s), seg(j, s), y_dn)
        g["share"] = []
        pass_on(j, s)

    def half_seg(j, s, half):
        return bufs[j]["ubuf"].at[core, s, :, pl.ds(half * mid, mid)]

    def cross(j, key, s):
        gats[j][key] = push(seg(j, s), seg(j, s), x_nb)

    def stage_y(j):
        g = gats[j]
        g["x"].wait_recv()
        s = own(0, 1 - x)
        if not x_first[j]:
            g["u1"] = push(seg(j, s), seg(j, s), y_up)
            g["d1"] = push(seg(j, s), seg(j, s), y_dn)
        pass_on(j, s)

    def stage_fwd(j):
        g = gats[j]
        if x_first[j]:
            g["u0"].wait_recv()
            below = own(3, x)
            g["fu"] = push(half_seg(j, below, 0), half_seg(j, below, 0), y_up)
            cross(j, "xb", below)
            pass_on(j, below)
            g["d0"].wait_recv()
            above = own(1, x)
            g["fd"] = push(half_seg(j, above, 1), half_seg(j, above, 1), y_dn)
            cross(j, "xa", above)
            pass_on(j, above)
            return
        g["u0"].wait_recv()
        below = own(3, x)
        g["fu"] = push(seg(j, below), seg(j, below), y_up)
        pass_on(j, below)
        g["d1"].wait_recv()
        above = own(1, 1 - x)
        g["fd"] = push(seg(j, above), seg(j, above), y_dn)
        pass_on(j, above)
        g["d0"].wait_recv()
        pass_on(j, own(1, x))
        g["u1"].wait_recv()
        pass_on(j, own(3, 1 - x))

    def stage_last(j):
        g = gats[j]
        g["fu"].wait_recv()
        if x_first[j]:
            g["fd"].wait_recv()
            cross(j, "xf", own(2, x))
            pass_on(j, own(2, x))
            g["xb"].wait_recv()
            pass_on(j, own(3, 1 - x))
            g["xa"].wait_recv()
            pass_on(j, own(1, 1 - x))
            return
        pass_on(j, own(2, x))
        g["fd"].wait_recv()
        pass_on(j, own(2, 1 - x))

    def stage_end(j):
        if x_first[j]:
            gats[j]["xf"].wait_recv()
            pass_on(j, own(2, 1 - x))

    def stage_out(j):
        ubuf = bufs[j]["ubuf"]
        at, h, _ = PARTS[j]
        for cp in gats[j]["share"]:
            cp.wait_recv()
        upd = mm_nt(ubuf[0].reshape(8 * h, block), sel[0]) + mm_nt(ubuf[1].reshape(8 * h, block), sel[1])
        for s in range(8):
            skip = 2 * SLAB - per_y if at == 0 and s % 2 == 1 else 0
            first = (s // 2) * per_y + (s % 2) * (per_y - SLAB) + at + skip
            rows = slice(first, first + h - skip)
            outv[rows, :] = coeffs[rows, :] + upd[s * h + skip:(s + 1) * h]

    stages = [stage_x, stage_swap, stage_u, stage_y, stage_fwd, stage_last, stage_end, stage_out]
    for t in range(n_parts + len(stages) - 1):
        for k, stage in enumerate(stages):
            if 0 <= t - k < n_parts:
                stage(t - k)

    for cp in sent:
        cp.wait_send()


def per_device(points, targets, coeffs, block_ids, inverses):
    local, feat = points.shape
    labels = targets.shape[1]
    block = block_ids.shape[1]
    n = 2 * block
    vm = pltpu.VMEM
    scratch = [
        vm((local, feat), BF16), vm((2, block), jnp.int32), vm((labels, local), BF16), vm((labels, local), F32), vm((2, block, block), F32),
        vm((labels, local), BF16), vm((2, local, block), BF16), vm((2, local, block), BF16),
        vm((2, 8, 64, LANES), BF16), vm((8, 64, LANES), BF16), vm((8, 64, LANES), BF16),
        vm((7, 64, LANES), BF16), vm((64, LANES), BF16), vm((8, n, LANES), BF16),
        vm((4, block, block), BF16), vm((local, 1), F32),
        pltpu.SemaphoreType.DMA((5,)),
        pltpu.SemaphoreType.DMA((COPIES,)), pltpu.SemaphoreType.DMA((COPIES,)),
    ]
    for _, h, x_first in PARTS:
        w = block // 2 if x_first else block
        crossing = (4, h, block) if x_first else (h, block)
        kept = crossing if x_first else (8, LANES)
        scratch += [
            vm((8, h, block), BF16), vm((8, h, block), F32), vm((8, h, block), BF16),
            vm((2, h, w), BF16), vm((2, h, w), BF16), vm((4, h, w), BF16), vm((2, 2, h, w), BF16),
            vm(crossing, BF16), vm(crossing, BF16), vm(kept, F32), vm((h, block), F32), vm((h, block), F32),
            vm((2, 8, h, block), BF16),
        ]
    in_vmem = pl.BlockSpec(memory_space=pltpu.VMEM)
    in_any = pl.BlockSpec(memory_space=pltpu.HBM)
    out = pl.pallas_call(
        body,
        out_shape=jax.ShapeDtypeStruct((labels, local), F32),
        in_specs=[in_any] * 5,
        out_specs=in_vmem,
        scratch_shapes=scratch,
        compiler_params=pltpu.CompilerParams(
            collective_id=0, has_side_effects=True, vmem_limit_bytes=44 << 20),
        name="descent",
    )(*[pltpu.with_memory_space_constraint(a, pltpu.HBM)
        for a in (points, block_ids, targets.T, coeffs.T, inverses)])
    return out.T


def solution(mesh):
    return jax.shard_map(
        per_device,
        mesh=mesh,
        in_specs=(P("rows", None), P("rows", "labels"), P("rows", "labels"), P(), P()),
        out_specs=P("rows", "labels"),
        check_vma=False,
    )
```

```python
import functools

import jax
import jax.numpy as jnp
from jax import lax
from jax.experimental import pallas as pl
from jax.experimental.pallas import tpu as pltpu
from jax.sharding import PartitionSpec as P

RIDGE = 0.5
MESH = pl.DeviceIdType.MESH
F32, BF16 = jnp.float32, jnp.bfloat16
LANES = 128
PARTS = ((0, 64), (64, 64), (128, 48))
SLAB = 176
COPIES = 176
NT = (((1,), (1,)), ((), ()))
TN = (((0,), (0,)), ((), ()))


def mm(a, b):
    return jnp.dot(a, b, preferred_element_type=F32)


def mm_nt(a, b):
    return lax.dot_general(a, b, NT, preferred_element_type=F32)


def split(x):
    hi = x.astype(BF16)
    return hi, (x - hi.astype(F32)).astype(BF16)


def one_hot(a, b):
    return jnp.where(a == b, 1.0, 0.0)


def row_norms(x):
    hi, lo = split(jnp.square(x.astype(F32)))
    ones = jnp.ones((8, x.shape[1]), BF16)
    return (mm_nt(ones, hi) + mm_nt(ones, lo))[0:1]


def col_norms(x):
    return jnp.sum(jnp.square(x.astype(F32)), axis=1, keepdims=True)


def gauss(left, left_norms, right, right_norms):
    dist = jnp.maximum(left_norms + right_norms - 2.0 * mm_nt(left, right), 0.0)
    return jnp.exp(-(2.0 / left.shape[1]) * dist).astype(BF16)


def body(points_hbm, ids_hbm, targets_hbm, coeffs_hbm, inverses_hbm, outv, *scratch):
    (points, ids, targets, coeffs, inverses, c_low, kt, sel, pick, qm, qx_recv, qchip, qr_recv, qpiece, qbuf,
     weights, point_norms, load_sem, send_sem, recv_sem) = scratch[:20]
    names = ("sums", "far", "rfar", "near", "rnear", "xs", "xr", "n_mine", "n_recv", "ubuf")
    bufs = [dict(zip(names, scratch[20 + len(names) * j: 20 + len(names) * (j + 1)])) for j in range(len(PARTS))]
    n_parts = len(PARTS)

    me = lax.axis_index("rows")
    lab = lax.axis_index("labels")
    core = me % 2
    chip = me // 2
    y = chip % 4
    x = chip // 4
    z = lab // 2
    xh = lab % 2
    block = ids_hbm.shape[1]
    local = points_hbm.shape[0]
    per_y = coeffs.shape[0] // 4

    def chip_peer(d):
        return {"rows": ((chip + d) % 8) * 2 + core}

    partner = {"rows": chip * 2 + 1 - core}
    y_up = {"rows": (x * 4 + (y + 1) % 4) * 2 + core}
    y_dn = {"rows": (x * 4 + (y + 3) % 4) * 2 + core}
    x_nb = {"rows": ((1 - x) * 4 + y) * 2 + core}
    z_up = {"labels": ((z + 1) % 8) * 2 + xh}
    z_dn = {"labels": ((z + 7) % 8) * 2 + xh}

    loads = [
        pltpu.make_async_copy(coeffs_hbm, coeffs, load_sem.at[0]),
        pltpu.make_async_copy(targets_hbm, targets.at[core], load_sem.at[1]),
        pltpu.make_async_copy(inverses_hbm, inverses, load_sem.at[2]),
        pltpu.make_async_copy(points_hbm, points.at[core], load_sem.at[3]),
        pltpu.make_async_copy(ids_hbm, ids, load_sem.at[4]),
    ]
    for ld in loads[::-1]:
        ld.start()

    barrier = pltpu.get_barrier_semaphore()
    greet = [partner, z_up, z_dn] + [chip_peer(d) for d in range(1, 8)]
    for dev in greet:
        pl.semaphore_signal(barrier, inc=1, device_id=dev, device_id_type=MESH)

    sent = []

    def push(src, dst, dev):
        i = len(sent)
        cp = pltpu.make_async_remote_copy(
            src_ref=src, dst_ref=dst, send_sem=send_sem.at[i], recv_sem=recv_sem.at[i],
            device_id=dev, device_id_type=MESH)
        cp.start()
        sent.append(cp)
        return cp

    first_row = me * local
    sub_row = first_row + lax.broadcasted_iota(jnp.int32, (local, 1), 0)

    loads[4].wait()
    loads[3].wait()
    z_lanes = pl.ds(pl.multiple_of((z // 2) * 128, 128), 128)
    z_half = pl.ds(pl.multiple_of((z % 2) * 64, 64), 64)
    for b in range(2):
        z_sel = one_hot(sub_row, ids[b:b + 1, z_lanes]).astype(BF16)
        found = lax.dot_general(z_sel, points[core], TN, preferred_element_type=F32).astype(BF16)
        for f in range(8):
            qm[b, f] = found[:, f * LANES:(f + 1) * LANES]
    pl.semaphore_wait(barrier, len(greet))
    qx = push(qm.at[1 - core, :, z_half, :], qx_recv, partner)
    lend_points = push(points.at[core], points.at[core], partner)
    my_ids = jnp.where(core == 0, ids[0:1, :], ids[1:2, :])
    for o in range(2):
        chip_row = (chip * 2 + o) * local + lax.broadcasted_iota(jnp.int32, (local, 1), 0)
        pick[o] = one_hot(chip_row, my_ids).astype(BF16)
    qx.wait_recv()
    qchip[...] = (qm[core, :, z_half, :].astype(F32) + qx_recv[...].astype(F32)).astype(BF16)
    red = [push(qchip.at[(chip + d) % 8], qr_recv.at[d - 1], chip_peer(d)) for d in range(1, 8)]

    piece = qchip[chip].astype(F32)
    for d in range(1, 8):
        red[d - 1].wait_recv()
        piece = piece + qr_recv[d - 1].astype(F32)
    qpiece[...] = piece.astype(BF16)
    zrows = pl.ds(pl.multiple_of(z * 64, 64), 64)
    qbuf[core, chip, zrows, :] = piece.astype(BF16)
    gat = [push(qpiece, qbuf.at[core, chip, zrows, :], chip_peer(d)) for d in range(1, 8)]
    loads[1].wait()
    lend_targets = push(targets.at[core], targets.at[core], partner)
    for cp in gat:
        cp.wait_recv()

    def zchunk(zz, at, n):
        rows = pl.ds(pl.multiple_of((zz % 8) * 64, 64), 64)
        return qbuf.at[core, pl.ds(at, n), rows, :]

    def block_points(b, start, size):
        return jnp.concatenate([qbuf[b, f, pl.ds(start, size), :] for f in range(8)], axis=1)

    def fill_tile(pair):
        at = pl.multiple_of((pair % 4) * 128, 128)
        q = block_points(core, at, 128)
        norms = row_norms(q)
        lanes = pl.ds(at, 128)
        for o in range(2):
            tile = gauss(points[o], point_norms[o], q, norms)
            kt[o, :, lanes] = (tile.astype(F32) + RIDGE * pick[o, :, lanes].astype(F32)).astype(BF16)

    pair = z // 2 + 4
    lean = 2 * (z % 2) - 1
    hops = {}
    for s in range(1, 5):
        for h in range(4):
            for sign, dev in ((1, z_up), (-1, z_dn)):
                held = z + 8 - sign * (s - 1)
                if s > 1:
                    hops[sign, s - 1, h].wait_recv()
                if s < 4 or (h < 2) == (sign == 1):
                    hops[sign, s, h] = push(zchunk(held, 2 * h, 2), zchunk(held, 2 * h, 2), dev)
        if s == 1:
            loads[0].wait()
            c_low[core] = coeffs[...].astype(BF16)
            lend_low = push(c_low.at[core], c_low.at[core], partner)
            lend_points.wait_recv()
            for o in range(2):
                point_norms[o] = col_norms(points[o])
        elif s == 2:
            fill_tile(pair)
            for b in range(2):
                sel[b] = one_hot(sub_row, ids[b:b + 1, :]).astype(BF16)
        elif s == 3:
            fill_tile(pair + lean)
        else:
            fill_tile(pair - lean)
    for sign, hs in ((1, (0, 1)), (-1, (2, 3))):
        for h in hs:
            hops[sign, 4, h].wait_recv()
    lend_block = push(qbuf.at[core], qbuf.at[core], partner)
    fill_tile(pair + 2)
    lend_targets.wait_recv()
    lend_low.wait_recv()

    def partial(st):
        rows = pl.ds(pl.multiple_of(((y + st) % 4) * per_y, 16), per_y)
        value = (mm(c_low[0, rows, :], kt[0]) + mm(c_low[1, rows, :], kt[1])
                 - mm(targets[0, rows, :], pick[0]) - mm(targets[1, rows, :], pick[1]))
        for j, (at, h) in enumerate(PARTS):
            for xx in range(2):
                off = xx * (per_y - SLAB) + at
                bufs[j]["sums"][pl.ds(((y + st) % 4) * 2 + xx, 1)] = value[off:off + h][None]

    reds = [dict() for _ in range(n_parts)]

    def chip_sum(j, st, xx):
        return bufs[j]["sums"][((y + st) % 4) * 2 + xx]

    partial(2)
    for j in range(n_parts):
        b, r = bufs[j], reds[j]
        for xx in range(2):
            b["far"][xx] = chip_sum(j, 2, xx).astype(BF16)
        r["fu"] = push(b["far"].at[0], b["rfar"].at[0], y_up)
        r["fd"] = push(b["far"].at[1], b["rfar"].at[1], y_dn)
    partial(1)
    partial(3)

    def stage_near(j):
        b, r = bufs[j], reds[j]
        b["near"][1] = chip_sum(j, 1, 1).astype(BF16)
        r["nu"] = push(b["near"].at[1], b["rnear"].at[0, 1], y_up)
        b["near"][2] = chip_sum(j, 3, 0).astype(BF16)
        r["nd"] = push(b["near"].at[2], b["rnear"].at[1, 0], y_dn)

    def stage_dep(j):
        b, r = bufs[j], reds[j]
        r["fu"].wait_recv()
        b["near"][0] = (chip_sum(j, 1, 0) + b["rfar"][0].astype(F32)).astype(BF16)
        r["du"] = push(b["near"].at[0], b["rnear"].at[0, 0], y_up)
        r["fd"].wait_recv()
        b["near"][3] = (chip_sum(j, 3, 1) + b["rfar"][1].astype(F32)).astype(BF16)
        r["dd"] = push(b["near"].at[3], b["rnear"].at[1, 1], y_dn)

    stage_near(0)
    partial(0)
    for j in range(n_parts):
        stage_dep(j)
        if j + 1 < n_parts:
            stage_near(j + 1)

    lend_block.wait_recv()
    q0, q1 = block_points(0, 0, block), block_points(1, 0, block)
    eye = lax.broadcasted_iota(jnp.int32, (block, block), 0) == lax.broadcasted_iota(jnp.int32, (block, block), 1)
    ids0 = jnp.sum(jnp.where(eye, ids[0:1, :].astype(F32), 0.0), axis=1, keepdims=True)
    same = one_hot(ids0, ids[1:2, :].astype(F32))
    cross = (gauss(q0, col_norms(q0), q1, row_norms(q1)).astype(F32) + RIDGE * same).astype(BF16)
    loads[2].wait()
    hi, lo = split(inverses[0])
    b_hi, b_lo = split(mm(hi, cross) + mm(lo, cross))
    hi, lo = split(inverses[1])
    c_hi, c_lo = split(jnp.where(core == 1, mm(b_hi, hi) + mm(b_hi, lo) + mm(b_lo, hi), 0.0))
    weights[2] = c_hi
    weights[3] = c_lo
    hi, lo = split(inverses[core])
    weights[0] = hi
    weights[1] = lo

    def own(step, xx):
        return ((y + step) % 4) * 2 + xx

    def seg(j, s):
        return bufs[j]["ubuf"].at[core, s]

    gats = [dict() for _ in range(n_parts)]

    def stage_x(j):
        b, r = bufs[j], reds[j]
        for key in ("nu", "nd", "du", "dd"):
            r[key].wait_recv()

        def total(xx):
            return chip_sum(j, 0, xx) + b["rnear"][0, xx].astype(F32) + b["rnear"][1, xx].astype(F32)

        b["xs"][...] = total(1 - x).astype(BF16)
        r["x"] = push(b["xs"], b["xr"], x_nb)
        b["n_mine"][...] = total(x)

    def stage_swap(j):
        b, r = bufs[j], reds[j]
        r["x"].wait_recv()
        b["n_mine"][...] = b["n_mine"][...] + b["xr"][...].astype(F32)
        r["swap"] = push(b["n_mine"], b["n_recv"], partner)

    def times(n, w_hi, w_lo):
        hi, lo = split(n)
        return mm(hi, w_hi) + mm(lo, w_hi) + mm(hi, w_lo)

    def pass_on(j, s):
        gats[j]["share"].append(push(seg(j, s), seg(j, s), partner))

    def stage_u(j):
        b, r, g = bufs[j], reds[j], gats[j]
        mine = times(b["n_mine"][...], weights[0], weights[1])
        r["swap"].wait_recv()
        u = times(b["n_recv"][...], weights[2], weights[3]) - mine
        s = own(0, x)
        b["ubuf"][core, s] = u.astype(BF16)
        g["x"] = push(seg(j, s), seg(j, s), x_nb)
        g["u0"] = push(seg(j, s), seg(j, s), y_up)
        g["d0"] = push(seg(j, s), seg(j, s), y_dn)
        g["share"] = []
        pass_on(j, s)

    def stage_y(j):
        g = gats[j]
        g["x"].wait_recv()
        s = own(0, 1 - x)
        g["u1"] = push(seg(j, s), seg(j, s), y_up)
        g["d1"] = push(seg(j, s), seg(j, s), y_dn)
        pass_on(j, s)

    def stage_fwd(j):
        g = gats[j]
        g["u0"].wait_recv()
        below = own(3, x)
        g["fu"] = push(seg(j, below), seg(j, below), y_up)
        pass_on(j, below)
        g["d1"].wait_recv()
        above = own(1, 1 - x)
        g["fd"] = push(seg(j, above), seg(j, above), y_dn)
        pass_on(j, above)
        g["d0"].wait_recv()
        pass_on(j, own(1, x))
        g["u1"].wait_recv()
        pass_on(j, own(3, 1 - x))

    def stage_last(j):
        g = gats[j]
        g["fu"].wait_recv()
        pass_on(j, own(2, x))
        g["fd"].wait_recv()
        pass_on(j, own(2, 1 - x))

    def stage_out(j):
        ubuf = bufs[j]["ubuf"]
        at, h = PARTS[j]
        for cp in gats[j]["share"]:
            cp.wait_recv()
        upd = mm_nt(ubuf[0].reshape(8 * h, block), sel[0]) + mm_nt(ubuf[1].reshape(8 * h, block), sel[1])
        for s in range(8):
            skip = 2 * SLAB - per_y if at == 0 and s % 2 == 1 else 0
            first = (s // 2) * per_y + (s % 2) * (per_y - SLAB) + at + skip
            rows = slice(first, first + h - skip)
            outv[rows, :] = coeffs[rows, :] + upd[s * h + skip:(s + 1) * h]

    stages = [stage_x, stage_swap, stage_u, stage_y, stage_fwd, stage_last, stage_out]
    for t in range(n_parts + len(stages) - 1):
        for k, stage in enumerate(stages):
            if 0 <= t - k < n_parts:
                stage(t - k)

    for cp in sent:
        cp.wait_send()


def per_device(points, targets, coeffs, block_ids, inverses):
    local, feat = points.shape
    labels = targets.shape[1]
    block = block_ids.shape[1]
    n = 2 * block
    vm = pltpu.VMEM
    scratch = [
        vm((2, local, feat), BF16), vm((2, block), jnp.int32), vm((2, labels, local), BF16), vm((labels, local), F32),
        vm((2, block, block), F32), vm((2, labels, local), BF16), vm((2, local, block), BF16), vm((2, local, block), BF16),
        vm((2, local, block), BF16), vm((2, 8, 128, LANES), BF16), vm((8, 64, LANES), BF16), vm((8, 64, LANES), BF16),
        vm((7, 64, LANES), BF16), vm((64, LANES), BF16), vm((2, 8, block, LANES), BF16),
        vm((4, block, block), BF16), vm((2, local, 1), F32),
        pltpu.SemaphoreType.DMA((5,)),
        pltpu.SemaphoreType.DMA((COPIES,)), pltpu.SemaphoreType.DMA((COPIES,)),
    ]
    for _, h in PARTS:
        scratch += [
            vm((8, h, block), F32),
            vm((2, h, block), BF16), vm((2, h, block), BF16), vm((4, h, block), BF16), vm((2, 2, h, block), BF16),
            vm((h, block), BF16), vm((h, block), BF16), vm((h, block), F32), vm((h, block), F32),
            vm((2, 8, h, block), BF16),
        ]
    in_vmem = pl.BlockSpec(memory_space=pltpu.VMEM)
    in_any = pl.BlockSpec(memory_space=pltpu.HBM)
    out = pl.pallas_call(
        body,
        out_shape=jax.ShapeDtypeStruct((labels, local), F32),
        in_specs=[in_any] * 5,
        out_specs=in_vmem,
        scratch_shapes=scratch,
        compiler_params=pltpu.CompilerParams(
            collective_id=0, has_side_effects=True, vmem_limit_bytes=44 << 20),
        name="descent",
    )(*[pltpu.with_memory_space_constraint(a, pltpu.HBM)
        for a in (points, block_ids, targets.T, coeffs.T, inverses)])
    return out.T


def solution(mesh):
    return jax.shard_map(
        per_device,
        mesh=mesh,
        in_specs=(P("rows", None), P("rows", "labels"), P("rows", "labels"), P(), P()),
        out_specs=P("rows", "labels"),
        check_vma=False,
    )
```

```python
import functools

import jax
import jax.numpy as jnp
from jax import lax
from jax.experimental import pallas as pl
from jax.experimental.pallas import tpu as pltpu
from jax.sharding import PartitionSpec as P

RIDGE = 0.5
MESH = pl.DeviceIdType.MESH
F32, BF16 = jnp.float32, jnp.bfloat16
LANES = 128
PARTS = ((0, 64), (64, 64), (128, 48))
SLAB = 176
COPIES = 176
NT = (((1,), (1,)), ((), ()))
TN = (((0,), (0,)), ((), ()))


def mm(a, b):
    return jnp.dot(a, b, preferred_element_type=F32)


def mm_nt(a, b):
    return lax.dot_general(a, b, NT, preferred_element_type=F32)


def split(x):
    hi = x.astype(BF16)
    return hi, (x - hi.astype(F32)).astype(BF16)


def one_hot(a, b):
    return jnp.where(a == b, 1.0, 0.0)


def row_norms(x):
    hi, lo = split(jnp.square(x.astype(F32)))
    ones = jnp.ones((8, x.shape[1]), BF16)
    return (mm_nt(ones, hi) + mm_nt(ones, lo))[0:1]


def col_norms(x):
    return jnp.sum(jnp.square(x.astype(F32)), axis=1, keepdims=True)


def gauss(left, left_norms, right, right_norms):
    dist = jnp.maximum(left_norms + right_norms - 2.0 * mm_nt(left, right), 0.0)
    return jnp.exp(-(2.0 / left.shape[1]) * dist).astype(BF16)


def body(points_hbm, ids_hbm, targets_hbm, coeffs_hbm, inverses_hbm, outv, *scratch):
    (points, ids, targets, coeffs, inverses, c_low, sel, qm, qx_recv, qchip, qr_recv, qpiece, qbuf,
     weights, point_norms, load_sem, near_sem, send_sem, recv_sem) = scratch[:19]
    names = ("kt", "pick", "sums", "far", "rfar", "near", "rnear", "xs", "xr", "n_mine", "n_recv")
    bufs = [dict(zip(names, scratch[19 + len(names) * p: 19 + len(names) * (p + 1)])) for p in range(2)]
    ubufs = scratch[19 + 2 * len(names):]
    n_parts = len(PARTS)

    me = lax.axis_index("rows")
    lab = lax.axis_index("labels")
    core = me % 2
    chip = me // 2
    y = chip % 4
    x = chip // 4
    z = lab // 2
    xh = lab % 2
    block = ids_hbm.shape[1]
    local = points_hbm.shape[0]
    per_y = coeffs.shape[0] // 4

    def chip_peer(d):
        return {"rows": ((chip + d) % 8) * 2 + core}

    partner = {"rows": chip * 2 + 1 - core}
    y_up = {"rows": (x * 4 + (y + 1) % 4) * 2 + core}
    y_dn = {"rows": (x * 4 + (y + 3) % 4) * 2 + core}
    def at_chip(xx, step):
        return {"rows": (xx * 4 + (y + step) % 4) * 2 + core}

    x_nb = {"rows": ((1 - x) * 4 + y) * 2 + core}
    z_up = {"labels": ((z + 1) % 8) * 2 + xh}
    z_dn = {"labels": ((z + 7) % 8) * 2 + xh}

    loads = [
        pltpu.make_async_copy(coeffs_hbm, coeffs, load_sem.at[0]),
        pltpu.make_async_copy(targets_hbm, targets.at[core], load_sem.at[1]),
        pltpu.make_async_copy(inverses_hbm, inverses, load_sem.at[2]),
        pltpu.make_async_copy(points_hbm, points.at[core], load_sem.at[3]),
        pltpu.make_async_copy(ids_hbm, ids, load_sem.at[4]),
    ]
    for ld in loads[::-1]:
        ld.start()

    barrier = pltpu.get_barrier_semaphore()
    greet = [partner, z_up, z_dn] + [chip_peer(d) for d in range(1, 8)]
    for dev in greet:
        pl.semaphore_signal(barrier, inc=1, device_id=dev, device_id_type=MESH)

    sent = []

    def push(src, dst, dev, slot=None):
        i = len(sent)
        cp = pltpu.make_async_remote_copy(
            src_ref=src, dst_ref=dst, send_sem=send_sem.at[i], recv_sem=recv_sem.at[i] if slot is None else near_sem.at[slot],
            device_id=dev, device_id_type=MESH)
        cp.start()
        sent.append(cp)
        return cp

    first_row = me * local
    sub_row = first_row + lax.broadcasted_iota(jnp.int32, (local, 1), 0)

    loads[4].wait()
    loads[3].wait()
    z_lanes = pl.ds(pl.multiple_of((z // 2) * 128, 128), 128)
    z_half = pl.ds(pl.multiple_of((z % 2) * 64, 64), 64)
    for b in range(2):
        z_sel = one_hot(sub_row, ids[b:b + 1, z_lanes]).astype(BF16)
        found = lax.dot_general(z_sel, points[core], TN, preferred_element_type=F32).astype(BF16)
        for f in range(8):
            qm[b, f] = found[:, f * LANES:(f + 1) * LANES]
    pl.semaphore_wait(barrier, len(greet))
    qx = push(qm.at[1 - core, :, z_half, :], qx_recv, partner)
    lend_points = push(points.at[core], points.at[core], partner)
    qx.wait_recv()
    qchip[...] = (qm[core, :, z_half, :].astype(F32) + qx_recv[...].astype(F32)).astype(BF16)
    red = [push(qchip.at[(chip + d) % 8], qr_recv.at[d - 1], chip_peer(d)) for d in range(1, 8)]

    piece = qchip[chip].astype(F32)
    for d in range(1, 8):
        red[d - 1].wait_recv()
        piece = piece + qr_recv[d - 1].astype(F32)
    qpiece[...] = piece.astype(BF16)
    zrows = pl.ds(pl.multiple_of(z * 64, 64), 64)
    qbuf[core, chip, zrows, :] = piece.astype(BF16)
    gat = [push(qpiece, qbuf.at[core, chip, zrows, :], chip_peer(d)) for d in range(1, 8)]
    loads[1].wait()
    lend_targets = push(targets.at[core], targets.at[core], partner)
    for cp in gat:
        cp.wait_recv()

    def zchunk(zz, at, n):
        rows = pl.ds(pl.multiple_of((zz % 8) * 64, 64), 64)
        return qbuf.at[core, pl.ds(at, n), rows, :]

    def block_points(b, start, size):
        return jnp.concatenate([qbuf[b, f, pl.ds(start, size), :] for f in range(8)], axis=1)

    def fill_tile(p, i, pair):
        at = pl.multiple_of((pair % 4) * 128, 128)
        q = block_points(core, at, 128)
        norms = row_norms(q)
        pair_ids = jnp.where(core == 0, ids[0:1, pl.ds(at, 128)], ids[1:2, pl.ds(at, 128)])
        for o in range(2):
            chip_row = (chip * 2 + o) * local + lax.broadcasted_iota(jnp.int32, (local, 1), 0)
            hit = one_hot(chip_row, pair_ids)
            tile = gauss(points[o], point_norms[o], q, norms)
            bufs[p]["kt"][o, :, i * 128:(i + 1) * 128] = (tile.astype(F32) + RIDGE * hit).astype(BF16)
            bufs[p]["pick"][o, :, i * 128:(i + 1) * 128] = hit.astype(BF16)

    reds = [dict() for _ in range(2)]

    def partial(p, st):
        b = bufs[p]
        rows = pl.ds(pl.multiple_of(((y + st) % 4) * per_y, 16), per_y)
        value = (mm(c_low[0, rows, :], b["kt"][0]) + mm(c_low[1, rows, :], b["kt"][1])
                 - mm(targets[0, rows, :], b["pick"][0]) - mm(targets[1, rows, :], b["pick"][1]))
        for xx in range(2):
            off = xx * (per_y - SLAB)
            b["sums"][pl.ds(((y + st) % 4) * 2 + xx, 1)] = value[off:off + SLAB][None]

    def chip_sum(p, st, xx):
        return bufs[p]["sums"][((y + st) % 4) * 2 + xx]

    def near(p, k, way, value, xx):
        b = bufs[p]
        b["near"][k] = value.astype(BF16)
        push(b["near"].at[k], b["rnear"].at[way, x], at_chip(xx, 1 if way == 0 else 3), 4 * p + 2 * way + x)

    def stage_far(p):
        b, r = bufs[p], reds[p]
        partial(p, 2)
        for xx in range(2):
            b["far"][xx] = chip_sum(p, 2, xx).astype(BF16)
        r["fu"] = push(b["far"].at[0], b["rfar"].at[0], y_up)
        r["fd"] = push(b["far"].at[1], b["rfar"].at[1], y_dn)

    def stage_near(p):
        b, r = bufs[p], reds[p]
        partial(p, 1)
        near(p, 1, 0, chip_sum(p, 1, 1), 1)
        partial(p, 3)
        near(p, 2, 1, chip_sum(p, 3, 0), 0)
        partial(p, 0)
        b["xs"][...] = chip_sum(p, 0, 1 - x).astype(BF16)
        r["x"] = push(b["xs"], b["xr"], x_nb)

    def stage_dep(p):
        b, r = bufs[p], reds[p]
        r["fu"].wait_recv()
        near(p, 0, 0, chip_sum(p, 1, 0) + b["rfar"][0].astype(F32), 0)
        r["fd"].wait_recv()
        near(p, 3, 1, chip_sum(p, 3, 1) + b["rfar"][1].astype(F32), 1)

    def stage_swap(p):
        b, r = bufs[p], reds[p]
        total = chip_sum(p, 0, x)
        r["x"].wait_recv()
        total = total + b["xr"][...].astype(F32)
        for way in range(2):
            for src in range(2):
                pltpu.make_async_remote_copy(
                    src_ref=b["near"].at[0], dst_ref=b["rnear"].at[way, src], send_sem=send_sem.at[0],
                    recv_sem=near_sem.at[4 * p + 2 * way + src], device_id=x_nb, device_id_type=MESH).wait_recv()
                total = total + b["rnear"][way, src].astype(F32)
        b["n_mine"][...] = total
        r["swap"] = push(b["n_mine"], b["n_recv"], partner)

    pair = z // 2 + 4
    lean = 2 * (z % 2) - 1
    hops = {}
    for s in range(1, 5):
        for h in range(4):
            for sign, dev in ((1, z_up), (-1, z_dn)):
                held = z + 8 - sign * (s - 1)
                if s > 1:
                    hops[sign, s - 1, h].wait_recv()
                if s < 4 or (h < 2) == (sign == 1):
                    hops[sign, s, h] = push(zchunk(held, 2 * h, 2), zchunk(held, 2 * h, 2), dev)
        if s == 1:
            loads[0].wait()
            c_low[core] = coeffs[...].astype(BF16)
            lend_low = push(c_low.at[core], c_low.at[core], partner)
            lend_points.wait_recv()
            for o in range(2):
                point_norms[o] = col_norms(points[o])
        elif s == 2:
            fill_tile(0, 0, pair)
            for b in range(2):
                sel[b] = one_hot(sub_row, ids[b:b + 1, :]).astype(BF16)
        elif s == 3:
            fill_tile(0, 1, pair + lean)
            lend_targets.wait_recv()
            lend_low.wait_recv()
            stage_far(0)
            stage_near(0)
        else:
            fill_tile(1, 0, pair - lean)
            stage_dep(0)
    for sign, hs in ((1, (0, 1)), (-1, (2, 3))):
        for h in hs:
            hops[sign, 4, h].wait_recv()
    lend_block = push(qbuf.at[core], qbuf.at[core], partner)
    fill_tile(1, 1, pair + 2)
    stage_far(1)
    stage_near(1)
    stage_swap(0)
    stage_dep(1)
    lend_block.wait_recv()

    q0, q1 = block_points(0, 0, block), block_points(1, 0, block)
    eye = lax.broadcasted_iota(jnp.int32, (block, block), 0) == lax.broadcasted_iota(jnp.int32, (block, block), 1)
    ids0 = jnp.sum(jnp.where(eye, ids[0:1, :].astype(F32), 0.0), axis=1, keepdims=True)
    same = one_hot(ids0, ids[1:2, :].astype(F32))
    cross = (gauss(q0, col_norms(q0), q1, row_norms(q1)).astype(F32) + RIDGE * same).astype(BF16)
    loads[2].wait()

    def arrival_rows(b):
        order = (pair, pair + lean, pair - lean, pair + 2)
        return jnp.concatenate(
            [inverses[b, pl.ds(pl.multiple_of((g % 4) * 128, 128), 128), :] for g in order], axis=0)

    hi, lo = split(arrival_rows(0))
    b_hi, b_lo = split(mm(hi, cross) + mm(lo, cross))
    hi, lo = split(inverses[1])
    c_hi, c_lo = split(jnp.where(core == 1, mm(b_hi, hi) + mm(b_hi, lo) + mm(b_lo, hi), 0.0))
    weights[2] = c_hi
    weights[3] = c_lo
    hi, lo = split(arrival_rows(core))
    weights[0] = hi
    weights[1] = lo

    def own(step, xx):
        return ((y + step) % 4) * 2 + xx

    def seg(j, s):
        return ubufs[j].at[core, s]

    gats = [dict() for _ in range(n_parts)]

    def times(n, w_hi, w_lo):
        hi, lo = split(n)
        return mm(hi, w_hi) + mm(lo, w_hi) + mm(hi, w_lo)

    def pass_on(j, s):
        gats[j]["share"].append(push(seg(j, s), seg(j, s), partner))

    stage_swap(1)

    def rows_of(j, name):
        at, h = PARTS[j]
        return jnp.concatenate([bufs[p][name][at:at + h, :] for p in range(2)], axis=1)

    def stage_u(j):
        g = gats[j]
        mine = times(rows_of(j, "n_mine"), weights[0], weights[1])
        if j == 0:
            for p in range(2):
                reds[p]["swap"].wait_recv()
        u = times(rows_of(j, "n_recv"), weights[2], weights[3]) - mine
        s = own(0, x)
        ubufs[j][core, s] = u.astype(BF16)
        g["x"] = push(seg(j, s), seg(j, s), x_nb)
        g["u0"] = push(seg(j, s), seg(j, s), y_up)
        g["d0"] = push(seg(j, s), seg(j, s), y_dn)
        g["u1"] = push(seg(j, s), seg(j, s), at_chip(1 - x, 1))
        g["d1"] = push(seg(j, s), seg(j, s), at_chip(1 - x, 3))
        g["share"] = []
        pass_on(j, s)

    def stage_y(j):
        g = gats[j]
        g["x"].wait_recv()
        s = own(0, 1 - x)
        pass_on(j, s)

    def stage_fwd(j):
        g = gats[j]
        g["u0"].wait_recv()
        below = own(3, x)
        g["fu"] = push(seg(j, below), seg(j, below), y_up)
        pass_on(j, below)
        g["d1"].wait_recv()
        above = own(1, 1 - x)
        g["fd"] = push(seg(j, above), seg(j, above), y_dn)
        pass_on(j, above)
        g["d0"].wait_recv()
        pass_on(j, own(1, x))
        g["u1"].wait_recv()
        pass_on(j, own(3, 1 - x))

    def stage_last(j):
        g = gats[j]
        g["fu"].wait_recv()
        pass_on(j, own(2, x))
        g["fd"].wait_recv()
        pass_on(j, own(2, 1 - x))

    def stage_out(j):
        ubuf = ubufs[j]
        at, h = PARTS[j]
        for cp in gats[j]["share"]:
            cp.wait_recv()
        upd = mm_nt(ubuf[0].reshape(8 * h, block), sel[0]) + mm_nt(ubuf[1].reshape(8 * h, block), sel[1])
        for s in range(8):
            skip = 2 * SLAB - per_y if at == 0 and s % 2 == 1 else 0
            first = (s // 2) * per_y + (s % 2) * (per_y - SLAB) + at + skip
            rows = slice(first, first + h - skip)
            outv[rows, :] = coeffs[rows, :] + upd[s * h + skip:(s + 1) * h]

    stages = [stage_u, stage_y, stage_fwd, stage_last, stage_out]
    for t in range(n_parts + len(stages) - 1):
        for k, stage in enumerate(stages):
            if 0 <= t - k < n_parts:
                stage(t - k)

    for cp in sent:
        cp.wait_send()


def per_device(points, targets, coeffs, block_ids, inverses):
    local, feat = points.shape
    labels = targets.shape[1]
    block = block_ids.shape[1]
    n = 2 * block
    vm = pltpu.VMEM
    scratch = [
        vm((2, local, feat), BF16), vm((2, block), jnp.int32), vm((2, labels, local), BF16), vm((labels, local), F32),
        vm((2, block, block), F32), vm((2, labels, local), BF16), vm((2, local, block), BF16),
        vm((2, 8, 128, LANES), BF16), vm((8, 64, LANES), BF16), vm((8, 64, LANES), BF16),
        vm((7, 64, LANES), BF16), vm((64, LANES), BF16), vm((2, 8, block, LANES), BF16),
        vm((4, block, block), BF16), vm((2, local, 1), F32),
        pltpu.SemaphoreType.DMA((5,)), pltpu.SemaphoreType.DMA((8,)),
        pltpu.SemaphoreType.DMA((COPIES,)), pltpu.SemaphoreType.DMA((COPIES,)),
    ]
    w = block // 2
    for _ in range(2):
        scratch += [
            vm((2, local, w), BF16), vm((2, local, w), BF16), vm((8, SLAB, w), F32),
            vm((2, SLAB, w), BF16), vm((2, SLAB, w), BF16), vm((4, SLAB, w), BF16), vm((2, 2, SLAB, w), BF16),
            vm((SLAB, w), BF16), vm((SLAB, w), BF16), vm((SLAB, w), F32), vm((SLAB, w), F32),
        ]
    scratch += [vm((2, 8, h, block), BF16) for _, h in PARTS]
    in_vmem = pl.BlockSpec(memory_space=pltpu.VMEM)
    in_any = pl.BlockSpec(memory_space=pltpu.HBM)
    out = pl.pallas_call(
        body,
        out_shape=jax.ShapeDtypeStruct((labels, local), F32),
        in_specs=[in_any] * 5,
        out_specs=in_vmem,
        scratch_shapes=scratch,
        compiler_params=pltpu.CompilerParams(
            collective_id=0, has_side_effects=True, vmem_limit_bytes=44 << 20),
        name="descent",
    )(*[pltpu.with_memory_space_constraint(a, pltpu.HBM)
        for a in (points, block_ids, targets.T, coeffs.T, inverses)])
    return out.T


def solution(mesh):
    return jax.shard_map(
        per_device,
        mesh=mesh,
        in_specs=(P("rows", None), P("rows", "labels"), P("rows", "labels"), P(), P()),
        out_specs=P("rows", "labels"),
        check_vma=False,
    )
```

```python
import functools

import jax
import jax.numpy as jnp
from jax import lax
from jax.experimental import pallas as pl
from jax.experimental.pallas import tpu as pltpu
from jax.sharding import PartitionSpec as P

RIDGE = 0.5
MESH = pl.DeviceIdType.MESH
F32, BF16 = jnp.float32, jnp.bfloat16
LANES = 128
PARTS = ((0, 64), (64, 64), (128, 48))
SLAB = 176
COPIES = 176
NT = (((1,), (1,)), ((), ()))
TN = (((0,), (0,)), ((), ()))


def mm(a, b):
    return jnp.dot(a, b, preferred_element_type=F32)


def mm_nt(a, b):
    return lax.dot_general(a, b, NT, preferred_element_type=F32)


def split(x):
    hi = x.astype(BF16)
    return hi, (x - hi.astype(F32)).astype(BF16)


def one_hot(a, b):
    return jnp.where(a == b, 1.0, 0.0)


def row_norms(x):
    hi, lo = split(jnp.square(x.astype(F32)))
    ones = jnp.ones((8, x.shape[1]), BF16)
    return (mm_nt(ones, hi) + mm_nt(ones, lo))[0:1]


def col_norms(x):
    return jnp.sum(jnp.square(x.astype(F32)), axis=1, keepdims=True)


def gauss(left, left_norms, right, right_norms):
    dist = jnp.maximum(left_norms + right_norms - 2.0 * mm_nt(left, right), 0.0)
    return jnp.exp(-(2.0 / left.shape[1]) * dist).astype(BF16)


def body(points_hbm, ids_hbm, targets_hbm, coeffs_hbm, inverses_hbm, outv, *scratch):
    (points, ids, targets, coeffs, inverses, c_low, sel, qm, qx_recv, qchip, qr_recv, qpiece, qbuf,
     weights, point_norms, load_sem, near_sem, send_sem, recv_sem) = scratch[:19]
    names = ("kt", "pick", "sums", "far", "rfar", "near", "rnear", "xs", "xr", "n_mine", "n_recv")
    bufs = [dict(zip(names, scratch[19 + len(names) * p: 19 + len(names) * (p + 1)])) for p in range(2)]
    ubufs = scratch[19 + 2 * len(names):]
    n_parts = len(PARTS)

    me = lax.axis_index("rows")
    lab = lax.axis_index("labels")
    core = me % 2
    chip = me // 2
    y = chip % 4
    x = chip // 4
    z = lab // 2
    xh = lab % 2
    block = ids_hbm.shape[1]
    local = points_hbm.shape[0]
    per_y = coeffs.shape[0] // 4

    def chip_peer(d):
        return {"rows": ((chip + d) % 8) * 2 + core}

    partner = {"rows": chip * 2 + 1 - core}
    y_up = {"rows": (x * 4 + (y + 1) % 4) * 2 + core}
    y_dn = {"rows": (x * 4 + (y + 3) % 4) * 2 + core}
    def at_chip(xx, step):
        return {"rows": (xx * 4 + (y + step) % 4) * 2 + core}

    x_nb = {"rows": ((1 - x) * 4 + y) * 2 + core}
    z_up = {"labels": ((z + 1) % 8) * 2 + xh}
    z_dn = {"labels": ((z + 7) % 8) * 2 + xh}

    loads = [
        pltpu.make_async_copy(coeffs_hbm, coeffs, load_sem.at[0]),
        pltpu.make_async_copy(targets_hbm, targets.at[core], load_sem.at[1]),
        pltpu.make_async_copy(inverses_hbm, inverses, load_sem.at[2]),
        pltpu.make_async_copy(points_hbm, points.at[core], load_sem.at[3]),
        pltpu.make_async_copy(ids_hbm, ids, load_sem.at[4]),
    ]
    loads[4].start()
    loads[3].start()

    barrier = pltpu.get_barrier_semaphore()
    greet = [partner, z_up, z_dn] + [chip_peer(d) for d in range(1, 8)]
    for dev in greet:
        pl.semaphore_signal(barrier, inc=1, device_id=dev, device_id_type=MESH)

    sent = []

    def push(src, dst, dev, slot=None):
        i = len(sent)
        cp = pltpu.make_async_remote_copy(
            src_ref=src, dst_ref=dst, send_sem=send_sem.at[i], recv_sem=recv_sem.at[i] if slot is None else near_sem.at[slot],
            device_id=dev, device_id_type=MESH)
        cp.start()
        sent.append(cp)
        return cp

    first_row = me * local
    sub_row = first_row + lax.broadcasted_iota(jnp.int32, (local, 1), 0)

    loads[4].wait()
    loads[3].wait()
    for ld in (loads[1], loads[0], loads[2]):
        ld.start()
    z_lanes = pl.ds(pl.multiple_of((z // 2) * 128, 128), 128)
    z_half = pl.ds(pl.multiple_of((z % 2) * 64, 64), 64)
    for b in range(2):
        z_sel = one_hot(sub_row, ids[b:b + 1, z_lanes]).astype(BF16)
        found = lax.dot_general(z_sel, points[core], TN, preferred_element_type=F32).astype(BF16)
        for f in range(8):
            qm[b, f] = found[:, f * LANES:(f + 1) * LANES]
    pl.semaphore_wait(barrier, len(greet))
    qx = push(qm.at[1 - core, :, z_half, :], qx_recv, partner)
    lend_points = push(points.at[core], points.at[core], partner)
    qx.wait_recv()
    qchip[...] = (qm[core, :, z_half, :].astype(F32) + qx_recv[...].astype(F32)).astype(BF16)
    red = [push(qchip.at[(chip + d) % 8], qr_recv.at[d - 1], chip_peer(d)) for d in range(1, 8)]

    piece = qchip[chip].astype(F32)
    for d in range(1, 8):
        red[d - 1].wait_recv()
        piece = piece + qr_recv[d - 1].astype(F32)
    qpiece[...] = piece.astype(BF16)
    zrows = pl.ds(pl.multiple_of(z * 64, 64), 64)
    qbuf[core, chip, zrows, :] = piece.astype(BF16)
    gat = [push(qpiece, qbuf.at[core, chip, zrows, :], chip_peer(d)) for d in range(1, 8)]
    loads[1].wait()
    lend_targets = push(targets.at[core], targets.at[core], partner)
    for cp in gat:
        cp.wait_recv()

    def zchunk(zz, at, n):
        rows = pl.ds(pl.multiple_of((zz % 8) * 64, 64), 64)
        return qbuf.at[core, pl.ds(at, n), rows, :]

    def block_points(b, start, size):
        return jnp.concatenate([qbuf[b, f, pl.ds(start, size), :] for f in range(8)], axis=1)

    def fill_tile(p, i, pair):
        at = pl.multiple_of((pair % 4) * 128, 128)
        q = block_points(core, at, 128)
        norms = row_norms(q)
        pair_ids = jnp.where(core == 0, ids[0:1, pl.ds(at, 128)], ids[1:2, pl.ds(at, 128)])
        for o in range(2):
            chip_row = (chip * 2 + o) * local + lax.broadcasted_iota(jnp.int32, (local, 1), 0)
            hit = one_hot(chip_row, pair_ids)
            tile = gauss(points[o], point_norms[o], q, norms)
            bufs[p]["kt"][o, :, i * 128:(i + 1) * 128] = (tile.astype(F32) + RIDGE * hit).astype(BF16)
            bufs[p]["pick"][o, :, i * 128:(i + 1) * 128] = hit.astype(BF16)

    reds = [dict() for _ in range(2)]

    def partial(p, st):
        b = bufs[p]
        rows = pl.ds(pl.multiple_of(((y + st) % 4) * per_y, 16), per_y)
        value = (mm(c_low[0, rows, :], b["kt"][0]) + mm(c_low[1, rows, :], b["kt"][1])
                 - mm(targets[0, rows, :], b["pick"][0]) - mm(targets[1, rows, :], b["pick"][1]))
        for xx in range(2):
            off = xx * (per_y - SLAB)
            b["sums"][pl.ds(((y + st) % 4) * 2 + xx, 1)] = value[off:off + SLAB][None]

    def chip_sum(p, st, xx):
        return bufs[p]["sums"][((y + st) % 4) * 2 + xx]

    def near(p, k, way, value, xx):
        b = bufs[p]
        b["near"][k] = value.astype(BF16)
        push(b["near"].at[k], b["rnear"].at[way, x], at_chip(xx, 1 if way == 0 else 3), 4 * p + 2 * way + x)

    def stage_far(p):
        b, r = bufs[p], reds[p]
        partial(p, 2)
        for xx in range(2):
            b["far"][xx] = chip_sum(p, 2, xx).astype(BF16)
        r["fu"] = push(b["far"].at[0], b["rfar"].at[0], y_up)
        r["fd"] = push(b["far"].at[1], b["rfar"].at[1], y_dn)

    def stage_near(p):
        b, r = bufs[p], reds[p]
        partial(p, 1)
        near(p, 1, 0, chip_sum(p, 1, 1), 1)
        partial(p, 3)
        near(p, 2, 1, chip_sum(p, 3, 0), 0)
        partial(p, 0)
        b["xs"][...] = chip_sum(p, 0, 1 - x).astype(BF16)
        r["x"] = push(b["xs"], b["xr"], x_nb)

    def stage_dep(p):
        b, r = bufs[p], reds[p]
        r["fu"].wait_recv()
        near(p, 0, 0, chip_sum(p, 1, 0) + b["rfar"][0].astype(F32), 0)
        r["fd"].wait_recv()
        near(p, 3, 1, chip_sum(p, 3, 1) + b["rfar"][1].astype(F32), 1)

    def stage_swap(p):
        b, r = bufs[p], reds[p]
        total = chip_sum(p, 0, x)
        r["x"].wait_recv()
        total = total + b["xr"][...].astype(F32)
        for way in range(2):
            for src in range(2):
                pltpu.make_async_remote_copy(
                    src_ref=b["near"].at[0], dst_ref=b["rnear"].at[way, src], send_sem=send_sem.at[0],
                    recv_sem=near_sem.at[4 * p + 2 * way + src], device_id=x_nb, device_id_type=MESH).wait_recv()
                total = total + b["rnear"][way, src].astype(F32)
        b["n_mine"][...] = total
        r["swap"] = push(b["n_mine"], b["n_recv"], partner)

    pair = z // 2 + 4
    lean = 2 * (z % 2) - 1
    def arrival_rows(b):
        order = (pair, pair + lean, pair - lean, pair + 2)
        return jnp.concatenate(
            [inverses[b, pl.ds(pl.multiple_of((g % 4) * 128, 128), 128), :] for g in order], axis=0)

    hops = {}
    for s in range(1, 5):
        for h in range(4):
            for sign, dev in ((1, z_up), (-1, z_dn)):
                held = z + 8 - sign * (s - 1)
                if s > 1:
                    hops[sign, s - 1, h].wait_recv()
                if s < 4 or (h < 2) == (sign == 1):
                    hops[sign, s, h] = push(zchunk(held, 2 * h, 2), zchunk(held, 2 * h, 2), dev)
        if s == 1:
            loads[0].wait()
            c_low[core] = coeffs[...].astype(BF16)
            lend_low = push(c_low.at[core], c_low.at[core], partner)
            lend_points.wait_recv()
            for o in range(2):
                point_norms[o] = col_norms(points[o])
        elif s == 2:
            fill_tile(0, 0, pair)
            loads[2].wait()
            hi, lo = split(arrival_rows(core))
            weights[0] = hi
            weights[1] = lo
            for b in range(2):
                sel[b] = one_hot(sub_row, ids[b:b + 1, :]).astype(BF16)
        elif s == 3:
            fill_tile(0, 1, pair + lean)
            lend_targets.wait_recv()
            lend_low.wait_recv()
            stage_far(0)
            stage_near(0)
        else:
            stage_dep(0)
            fill_tile(1, 0, pair - lean)
    for sign, hs in ((1, (0, 1)), (-1, (2, 3))):
        for h in hs:
            hops[sign, 4, h].wait_recv()
    lend_block = push(qbuf.at[core], qbuf.at[core], partner)
    fill_tile(1, 1, pair + 2)
    stage_far(1)
    stage_near(1)
    stage_swap(0)
    stage_dep(1)
    lend_block.wait_recv()

    q0, q1 = block_points(0, 0, block), block_points(1, 0, block)
    eye = lax.broadcasted_iota(jnp.int32, (block, block), 0) == lax.broadcasted_iota(jnp.int32, (block, block), 1)
    ids0 = jnp.sum(jnp.where(eye, ids[0:1, :].astype(F32), 0.0), axis=1, keepdims=True)
    same = one_hot(ids0, ids[1:2, :].astype(F32))
    cross = (gauss(q0, col_norms(q0), q1, row_norms(q1)).astype(F32) + RIDGE * same).astype(BF16)
    hi, lo = split(arrival_rows(0))
    b_hi, b_lo = split(mm(hi, cross) + mm(lo, cross))
    hi, lo = split(inverses[1])
    c_hi, c_lo = split(jnp.where(core == 1, mm(b_hi, hi) + mm(b_hi, lo) + mm(b_lo, hi), 0.0))
    weights[2] = c_hi
    weights[3] = c_lo

    def own(step, xx):
        return ((y + step) % 4) * 2 + xx

    def seg(j, s):
        return ubufs[j].at[core, s]

    gats = [dict() for _ in range(n_parts)]

    def times(n, w_hi, w_lo):
        hi, lo = split(n)
        both = mm(jnp.concatenate([hi, lo], axis=0), w_hi)
        return both[:n.shape[0]] + both[n.shape[0]:] + mm(hi, w_lo)

    def pass_on(j, s):
        gats[j]["share"].append(push(seg(j, s), seg(j, s), partner))

    stage_swap(1)

    def rows_of(j, name):
        at, h = PARTS[j]
        return jnp.concatenate([bufs[p][name][at:at + h, :] for p in range(2)], axis=1)

    def stage_u(j):
        g = gats[j]
        mine = times(rows_of(j, "n_mine"), weights[0], weights[1])
        if j == 0:
            for p in range(2):
                reds[p]["swap"].wait_recv()
        u = times(rows_of(j, "n_recv"), weights[2], weights[3]) - mine
        s = own(0, x)
        ubufs[j][core, s] = u.astype(BF16)
        g["x"] = push(seg(j, s), seg(j, s), x_nb)
        g["u0"] = push(seg(j, s), seg(j, s), y_up)
        g["d0"] = push(seg(j, s), seg(j, s), y_dn)
        g["u1"] = push(seg(j, s), seg(j, s), at_chip(1 - x, 1))
        g["d1"] = push(seg(j, s), seg(j, s), at_chip(1 - x, 3))
        g["share"] = []
        pass_on(j, s)

    def stage_y(j):
        g = gats[j]
        g["x"].wait_recv()
        s = own(0, 1 - x)
        pass_on(j, s)

    def stage_fwd(j):
        g = gats[j]
        g["u0"].wait_recv()
        below = own(3, x)
        g["fu"] = push(seg(j, below), seg(j, below), y_up)
        pass_on(j, below)
        g["d1"].wait_recv()
        above = own(1, 1 - x)
        g["fd"] = push(seg(j, above), seg(j, above), y_dn)
        pass_on(j, above)
        g["d0"].wait_recv()
        pass_on(j, own(1, x))
        g["u1"].wait_recv()
        pass_on(j, own(3, 1 - x))

    def stage_last(j):
        g = gats[j]
        g["fu"].wait_recv()
        pass_on(j, own(2, x))
        g["fd"].wait_recv()
        pass_on(j, own(2, 1 - x))

    def stage_out(j):
        ubuf = ubufs[j]
        at, h = PARTS[j]
        for cp in gats[j]["share"]:
            cp.wait_recv()
        upd = mm_nt(ubuf[0].reshape(8 * h, block), sel[0]) + mm_nt(ubuf[1].reshape(8 * h, block), sel[1])
        for s in range(8):
            skip = 2 * SLAB - per_y if at == 0 and s % 2 == 1 else 0
            first = (s // 2) * per_y + (s % 2) * (per_y - SLAB) + at + skip
            rows = slice(first, first + h - skip)
            outv[rows, :] = coeffs[rows, :] + upd[s * h + skip:(s + 1) * h]

    stages = [stage_u, stage_y, stage_fwd, stage_last, stage_out]
    for t in range(n_parts + len(stages) - 1):
        for k, stage in enumerate(stages):
            if 0 <= t - k < n_parts:
                stage(t - k)

    for cp in sent:
        cp.wait_send()


def per_device(points, targets, coeffs, block_ids, inverses):
    local, feat = points.shape
    labels = targets.shape[1]
    block = block_ids.shape[1]
    n = 2 * block
    vm = pltpu.VMEM
    scratch = [
        vm((2, local, feat), BF16), vm((2, block), jnp.int32), vm((2, labels, local), BF16), vm((labels, local), F32),
        vm((2, block, block), F32), vm((2, labels, local), BF16), vm((2, local, block), BF16),
        vm((2, 8, 128, LANES), BF16), vm((8, 64, LANES), BF16), vm((8, 64, LANES), BF16),
        vm((7, 64, LANES), BF16), vm((64, LANES), BF16), vm((2, 8, block, LANES), BF16),
        vm((4, block, block), BF16), vm((2, local, 1), F32),
        pltpu.SemaphoreType.DMA((5,)), pltpu.SemaphoreType.DMA((8,)),
        pltpu.SemaphoreType.DMA((COPIES,)), pltpu.SemaphoreType.DMA((COPIES,)),
    ]
    w = block // 2
    for _ in range(2):
        scratch += [
            vm((2, local, w), BF16), vm((2, local, w), BF16), vm((8, SLAB, w), F32),
            vm((2, SLAB, w), BF16), vm((2, SLAB, w), BF16), vm((4, SLAB, w), BF16), vm((2, 2, SLAB, w), BF16),
            vm((SLAB, w), BF16), vm((SLAB, w), BF16), vm((SLAB, w), F32), vm((SLAB, w), F32),
        ]
    scratch += [vm((2, 8, h, block), BF16) for _, h in PARTS]
    in_vmem = pl.BlockSpec(memory_space=pltpu.VMEM)
    in_any = pl.BlockSpec(memory_space=pltpu.HBM)
    out = pl.pallas_call(
        body,
        out_shape=jax.ShapeDtypeStruct((labels, local), F32),
        in_specs=[in_any] * 5,
        out_specs=in_vmem,
        scratch_shapes=scratch,
        compiler_params=pltpu.CompilerParams(
            collective_id=0, has_side_effects=True, vmem_limit_bytes=44 << 20),
        name="descent",
    )(*[pltpu.with_memory_space_constraint(a, pltpu.HBM)
        for a in (points, block_ids, targets.T, coeffs.T, inverses)])
    return out.T


def solution(mesh):
    return jax.shard_map(
        per_device,
        mesh=mesh,
        in_specs=(P("rows", None), P("rows", "labels"), P("rows", "labels"), P(), P()),
        out_specs=P("rows", "labels"),
        check_vma=False,
    )
```

```python
import functools

import jax
import jax.numpy as jnp
from jax import lax
from jax.experimental import pallas as pl
from jax.experimental.pallas import tpu as pltpu
from jax.sharding import PartitionSpec as P

RIDGE = 0.5
MESH = pl.DeviceIdType.MESH
F32, BF16 = jnp.float32, jnp.bfloat16
LANES = 128
PARTS = ((0, 48), (48, 48), (96, 48), (144, 32))
SLAB = 176
COPIES = 200
NT = (((1,), (1,)), ((), ()))
TN = (((0,), (0,)), ((), ()))


def mm(a, b):
    return jnp.dot(a, b, preferred_element_type=F32)


def mm_nt(a, b):
    return lax.dot_general(a, b, NT, preferred_element_type=F32)


def split(x):
    hi = x.astype(BF16)
    return hi, (x - hi.astype(F32)).astype(BF16)


def one_hot(a, b):
    return jnp.where(a == b, 1.0, 0.0)


def row_norms(x):
    hi, lo = split(jnp.square(x.astype(F32)))
    ones = jnp.ones((8, x.shape[1]), BF16)
    return (mm_nt(ones, hi) + mm_nt(ones, lo))[0:1]


def col_norms(x):
    return jnp.sum(jnp.square(x.astype(F32)), axis=1, keepdims=True)


def gauss(left, left_norms, right, right_norms):
    dist = jnp.maximum(left_norms + right_norms - 2.0 * mm_nt(left, right), 0.0)
    return jnp.exp(-(2.0 / left.shape[1]) * dist).astype(BF16)


def body(points_hbm, ids_hbm, targets_hbm, coeffs_hbm, inverses_hbm, outv, *scratch):
    (points, ids, targets, coeffs, inverses, c_low, sel, qm, qx_recv, qchip, qr_recv, qpiece, qbuf,
     weights, point_norms, load_sem, near_sem, send_sem, recv_sem) = scratch[:19]
    names = ("kt", "pick", "sums", "far", "rfar", "near", "rnear", "xs", "xr", "n_mine", "n_recv")
    bufs = [dict(zip(names, scratch[19 + len(names) * p: 19 + len(names) * (p + 1)])) for p in range(2)]
    ubufs = scratch[19 + 2 * len(names):]
    n_parts = len(PARTS)

    me = lax.axis_index("rows")
    lab = lax.axis_index("labels")
    core = me % 2
    chip = me // 2
    y = chip % 4
    x = chip // 4
    z = lab // 2
    xh = lab % 2
    block = ids_hbm.shape[1]
    local = points_hbm.shape[0]
    per_y = coeffs.shape[0] // 4

    def chip_peer(d):
        return {"rows": ((chip + d) % 8) * 2 + core}

    partner = {"rows": chip * 2 + 1 - core}
    y_up = {"rows": (x * 4 + (y + 1) % 4) * 2 + core}
    y_dn = {"rows": (x * 4 + (y + 3) % 4) * 2 + core}
    def at_chip(xx, step):
        return {"rows": (xx * 4 + (y + step) % 4) * 2 + core}

    x_nb = {"rows": ((1 - x) * 4 + y) * 2 + core}
    z_up = {"labels": ((z + 1) % 8) * 2 + xh}
    z_dn = {"labels": ((z + 7) % 8) * 2 + xh}

    loads = [
        pltpu.make_async_copy(coeffs_hbm, coeffs, load_sem.at[0]),
        pltpu.make_async_copy(targets_hbm, targets.at[core], load_sem.at[1]),
        pltpu.make_async_copy(inverses_hbm, inverses, load_sem.at[2]),
        pltpu.make_async_copy(points_hbm, points.at[core], load_sem.at[3]),
        pltpu.make_async_copy(ids_hbm, ids, load_sem.at[4]),
    ]
    loads[4].start()
    loads[3].start()

    barrier = pltpu.get_barrier_semaphore()
    greet = [partner, z_up, z_dn] + [chip_peer(d) for d in range(1, 8)]
    for dev in greet:
        pl.semaphore_signal(barrier, inc=1, device_id=dev, device_id_type=MESH)

    sent = []

    def push(src, dst, dev, slot=None):
        i = len(sent)
        cp = pltpu.make_async_remote_copy(
            src_ref=src, dst_ref=dst, send_sem=send_sem.at[i], recv_sem=recv_sem.at[i] if slot is None else near_sem.at[slot],
            device_id=dev, device_id_type=MESH)
        cp.start()
        sent.append(cp)
        return cp

    first_row = me * local
    sub_row = first_row + lax.broadcasted_iota(jnp.int32, (local, 1), 0)

    loads[4].wait()
    loads[3].wait()
    for ld in (loads[1], loads[0], loads[2]):
        ld.start()
    z_lanes = pl.ds(pl.multiple_of((z // 2) * 128, 128), 128)
    z_half = pl.ds(pl.multiple_of((z % 2) * 64, 64), 64)
    for b in range(2):
        z_sel = one_hot(sub_row, ids[b:b + 1, z_lanes]).astype(BF16)
        found = lax.dot_general(z_sel, points[core], TN, preferred_element_type=F32).astype(BF16)
        for f in range(8):
            qm[b, f] = found[:, f * LANES:(f + 1) * LANES]
    pl.semaphore_wait(barrier, len(greet))
    qx = push(qm.at[1 - core, :, z_half, :], qx_recv, partner)
    lend_points = push(points.at[core], points.at[core], partner)
    qx.wait_recv()
    qchip[...] = (qm[core, :, z_half, :].astype(F32) + qx_recv[...].astype(F32)).astype(BF16)
    red = [push(qchip.at[(chip + d) % 8], qr_recv.at[d - 1], chip_peer(d)) for d in range(1, 8)]

    piece = qchip[chip].astype(F32)
    for d in range(1, 8):
        red[d - 1].wait_recv()
        piece = piece + qr_recv[d - 1].astype(F32)
    qpiece[...] = piece.astype(BF16)
    zrows = pl.ds(pl.multiple_of(z * 64, 64), 64)
    qbuf[core, chip, zrows, :] = piece.astype(BF16)
    gat = [push(qpiece, qbuf.at[core, chip, zrows, :], chip_peer(d)) for d in range(1, 8)]
    loads[1].wait()
    lend_targets = push(targets.at[core], targets.at[core], partner)
    for cp in gat:
        cp.wait_recv()

    def zchunk(zz, at, n):
        rows = pl.ds(pl.multiple_of((zz % 8) * 64, 64), 64)
        return qbuf.at[core, pl.ds(at, n), rows, :]

    def block_points(b, start, size):
        return jnp.concatenate([qbuf[b, f, pl.ds(start, size), :] for f in range(8)], axis=1)

    def fill_tile(p, i, pair):
        at = pl.multiple_of((pair % 4) * 128, 128)
        q = block_points(core, at, 128)
        norms = row_norms(q)
        pair_ids = jnp.where(core == 0, ids[0:1, pl.ds(at, 128)], ids[1:2, pl.ds(at, 128)])
        for o in range(2):
            chip_row = (chip * 2 + o) * local + lax.broadcasted_iota(jnp.int32, (local, 1), 0)
            hit = one_hot(chip_row, pair_ids)
            tile = gauss(points[o], point_norms[o], q, norms)
            bufs[p]["kt"][o, :, i * 128:(i + 1) * 128] = (tile.astype(F32) + RIDGE * hit).astype(BF16)
            bufs[p]["pick"][o, :, i * 128:(i + 1) * 128] = hit.astype(BF16)

    reds = [dict() for _ in range(2)]

    def partial(p, st):
        b = bufs[p]
        rows = pl.ds(pl.multiple_of(((y + st) % 4) * per_y, 16), per_y)
        value = (mm(c_low[0, rows, :], b["kt"][0]) + mm(c_low[1, rows, :], b["kt"][1])
                 - mm(targets[0, rows, :], b["pick"][0]) - mm(targets[1, rows, :], b["pick"][1]))
        for xx in range(2):
            off = xx * (per_y - SLAB)
            b["sums"][pl.ds(((y + st) % 4) * 2 + xx, 1)] = value[off:off + SLAB][None]

    def chip_sum(p, st, xx):
        return bufs[p]["sums"][((y + st) % 4) * 2 + xx]

    def near(p, k, way, value, xx):
        b = bufs[p]
        b["near"][k] = value.astype(BF16)
        push(b["near"].at[k], b["rnear"].at[way, x], at_chip(xx, 1 if way == 0 else 3), 4 * p + 2 * way + x)

    def stage_far(p):
        b, r = bufs[p], reds[p]
        partial(p, 2)
        for xx in range(2):
            b["far"][xx] = chip_sum(p, 2, xx).astype(BF16)
        r["fu"] = push(b["far"].at[0], b["rfar"].at[0], y_up)
        r["fd"] = push(b["far"].at[1], b["rfar"].at[1], y_dn)

    def stage_near(p):
        b, r = bufs[p], reds[p]
        partial(p, 1)
        near(p, 1, 0, chip_sum(p, 1, 1), 1)
        partial(p, 3)
        near(p, 2, 1, chip_sum(p, 3, 0), 0)
        partial(p, 0)
        b["xs"][...] = chip_sum(p, 0, 1 - x).astype(BF16)
        r["x"] = push(b["xs"], b["xr"], x_nb)

    def stage_dep(p):
        b, r = bufs[p], reds[p]
        r["fu"].wait_recv()
        near(p, 0, 0, chip_sum(p, 1, 0) + b["rfar"][0].astype(F32), 0)
        r["fd"].wait_recv()
        near(p, 3, 1, chip_sum(p, 3, 1) + b["rfar"][1].astype(F32), 1)

    def stage_swap(p):
        b, r = bufs[p], reds[p]
        total = chip_sum(p, 0, x)
        r["x"].wait_recv()
        total = total + b["xr"][...].astype(F32)
        for way in range(2):
            for src in range(2):
                pltpu.make_async_remote_copy(
                    src_ref=b["near"].at[0], dst_ref=b["rnear"].at[way, src], send_sem=send_sem.at[0],
                    recv_sem=near_sem.at[4 * p + 2 * way + src], device_id=x_nb, device_id_type=MESH).wait_recv()
                total = total + b["rnear"][way, src].astype(F32)
        b["n_mine"][...] = total
        r["swap"] = push(b["n_mine"], b["n_recv"], partner)

    pair = z // 2 + 4
    lean = 2 * (z % 2) - 1
    def arrival_rows(b):
        order = (pair, pair + lean, pair - lean, pair + 2)
        return jnp.concatenate(
            [inverses[b, pl.ds(pl.multiple_of((g % 4) * 128, 128), 128), :] for g in order], axis=0)

    hops = {}
    for s in range(1, 5):
        for h in range(4):
            for sign, dev in ((1, z_up), (-1, z_dn)):
                held = z + 8 - sign * (s - 1)
                if s > 1:
                    hops[sign, s - 1, h].wait_recv()
                if s < 4 or (h < 2) == (sign == 1):
                    hops[sign, s, h] = push(zchunk(held, 2 * h, 2), zchunk(held, 2 * h, 2), dev)
        if s == 1:
            loads[0].wait()
            c_low[core] = coeffs[...].astype(BF16)
            lend_low = push(c_low.at[core], c_low.at[core], partner)
            lend_points.wait_recv()
            for o in range(2):
                point_norms[o] = col_norms(points[o])
        elif s == 2:
            fill_tile(0, 0, pair)
            loads[2].wait()
            hi, lo = split(arrival_rows(core))
            weights[0] = hi
            weights[1] = lo
            for b in range(2):
                sel[b] = one_hot(sub_row, ids[b:b + 1, :]).astype(BF16)
        elif s == 3:
            fill_tile(0, 1, pair + lean)
            lend_targets.wait_recv()
            lend_low.wait_recv()
            stage_far(0)
            stage_near(0)
        else:
            stage_dep(0)
            fill_tile(1, 0, pair - lean)
    for sign, hs in ((1, (0, 1)), (-1, (2, 3))):
        for h in hs:
            hops[sign, 4, h].wait_recv()
    lend_block = push(qbuf.at[core], qbuf.at[core], partner)
    fill_tile(1, 1, pair + 2)
    stage_far(1)
    stage_near(1)
    stage_swap(0)
    stage_dep(1)
    lend_block.wait_recv()

    q0, q1 = block_points(0, 0, block), block_points(1, 0, block)
    eye = lax.broadcasted_iota(jnp.int32, (block, block), 0) == lax.broadcasted_iota(jnp.int32, (block, block), 1)
    ids0 = jnp.sum(jnp.where(eye, ids[0:1, :].astype(F32), 0.0), axis=1, keepdims=True)
    same = one_hot(ids0, ids[1:2, :].astype(F32))
    cross = (gauss(q0, col_norms(q0), q1, row_norms(q1)).astype(F32) + RIDGE * same).astype(BF16)
    hi, lo = split(arrival_rows(0))
    b_hi, b_lo = split(mm(hi, cross) + mm(lo, cross))
    hi, lo = split(inverses[1])
    c_hi, c_lo = split(jnp.where(core == 1, mm(b_hi, hi) + mm(b_hi, lo) + mm(b_lo, hi), 0.0))
    weights[2] = c_hi
    weights[3] = c_lo

    def own(step, xx):
        return ((y + step) % 4) * 2 + xx

    def seg(j, s):
        return ubufs[j].at[core, s]

    gats = [dict() for _ in range(n_parts)]

    def times(n, w_hi, w_lo):
        hi, lo = split(n)
        both = mm(jnp.concatenate([hi, lo], axis=0), w_hi)
        return both[:n.shape[0]] + both[n.shape[0]:] + mm(hi, w_lo)

    def pass_on(j, s):
        gats[j]["share"].append(push(seg(j, s), seg(j, s), partner))

    stage_swap(1)

    def rows_of(j, name):
        at, h = PARTS[j]
        return jnp.concatenate([bufs[p][name][at:at + h, :] for p in range(2)], axis=1)

    def stage_u(j):
        g = gats[j]
        mine = times(rows_of(j, "n_mine"), weights[0], weights[1])
        if j == 0:
            for p in range(2):
                reds[p]["swap"].wait_recv()
        u = times(rows_of(j, "n_recv"), weights[2], weights[3]) - mine
        s = own(0, x)
        ubufs[j][core, s] = u.astype(BF16)
        g["x"] = push(seg(j, s), seg(j, s), x_nb)
        g["u0"] = push(seg(j, s), seg(j, s), y_up)
        g["d0"] = push(seg(j, s), seg(j, s), y_dn)
        g["u1"] = push(seg(j, s), seg(j, s), at_chip(1 - x, 1))
        g["d1"] = push(seg(j, s), seg(j, s), at_chip(1 - x, 3))
        g["share"] = []
        pass_on(j, s)

    def stage_y(j):
        g = gats[j]
        g["x"].wait_recv()
        s = own(0, 1 - x)
        pass_on(j, s)

    def stage_fwd(j):
        g = gats[j]
        g["u0"].wait_recv()
        below = own(3, x)
        g["fu"] = push(seg(j, below), seg(j, below), y_up)
        pass_on(j, below)
        g["d1"].wait_recv()
        above = own(1, 1 - x)
        g["fd"] = push(seg(j, above), seg(j, above), y_dn)
        pass_on(j, above)
        g["d0"].wait_recv()
        pass_on(j, own(1, x))
        g["u1"].wait_recv()
        pass_on(j, own(3, 1 - x))

    def stage_last(j):
        g = gats[j]
        g["fu"].wait_recv()
        pass_on(j, own(2, x))
        g["fd"].wait_recv()
        pass_on(j, own(2, 1 - x))

    def stage_out(j):
        ubuf = ubufs[j]
        at, h = PARTS[j]
        for cp in gats[j]["share"]:
            cp.wait_recv()
        upd = mm_nt(ubuf[0].reshape(8 * h, block), sel[0]) + mm_nt(ubuf[1].reshape(8 * h, block), sel[1])
        for s in range(8):
            skip = 2 * SLAB - per_y if at == 0 and s % 2 == 1 else 0
            first = (s // 2) * per_y + (s % 2) * (per_y - SLAB) + at + skip
            rows = slice(first, first + h - skip)
            outv[rows, :] = coeffs[rows, :] + upd[s * h + skip:(s + 1) * h]

    stages = [stage_u, stage_y, stage_fwd, stage_last, stage_out]
    for t in range(n_parts + len(stages) - 1):
        for k, stage in enumerate(stages):
            if 0 <= t - k < n_parts:
                stage(t - k)

    for cp in sent:
        cp.wait_send()


def per_device(points, targets, coeffs, block_ids, inverses):
    local, feat = points.shape
    labels = targets.shape[1]
    block = block_ids.shape[1]
    n = 2 * block
    vm = pltpu.VMEM
    scratch = [
        vm((2, local, feat), BF16), vm((2, block), jnp.int32), vm((2, labels, local), BF16), vm((labels, local), F32),
        vm((2, block, block), F32), vm((2, labels, local), BF16), vm((2, local, block), BF16),
        vm((2, 8, 128, LANES), BF16), vm((8, 64, LANES), BF16), vm((8, 64, LANES), BF16),
        vm((7, 64, LANES), BF16), vm((64, LANES), BF16), vm((2, 8, block, LANES), BF16),
        vm((4, block, block), BF16), vm((2, local, 1), F32),
        pltpu.SemaphoreType.DMA((5,)), pltpu.SemaphoreType.DMA((8,)),
        pltpu.SemaphoreType.DMA((COPIES,)), pltpu.SemaphoreType.DMA((COPIES,)),
    ]
    w = block // 2
    for _ in range(2):
        scratch += [
            vm((2, local, w), BF16), vm((2, local, w), BF16), vm((8, SLAB, w), F32),
            vm((2, SLAB, w), BF16), vm((2, SLAB, w), BF16), vm((4, SLAB, w), BF16), vm((2, 2, SLAB, w), BF16),
            vm((SLAB, w), BF16), vm((SLAB, w), BF16), vm((SLAB, w), F32), vm((SLAB, w), F32),
        ]
    scratch += [vm((2, 8, h, block), BF16) for _, h in PARTS]
    in_vmem = pl.BlockSpec(memory_space=pltpu.VMEM)
    in_any = pl.BlockSpec(memory_space=pltpu.HBM)
    out = pl.pallas_call(
        body,
        out_shape=jax.ShapeDtypeStruct((labels, local), F32),
        in_specs=[in_any] * 5,
        out_specs=in_vmem,
        scratch_shapes=scratch,
        compiler_params=pltpu.CompilerParams(
            collective_id=0, has_side_effects=True, vmem_limit_bytes=44 << 20),
        name="descent",
    )(*[pltpu.with_memory_space_constraint(a, pltpu.HBM)
        for a in (points, block_ids, targets.T, coeffs.T, inverses)])
    return out.T


def solution(mesh):
    return jax.shard_map(
        per_device,
        mesh=mesh,
        in_specs=(P("rows", None), P("rows", "labels"), P("rows", "labels"), P(), P()),
        out_specs=P("rows", "labels"),
        check_vma=False,
    )
```
